128 devices in a mesh: groups: 4 (over x), shard: 32 (over y, z, core).
Axes of the slice: x: 4, y: 4, z: 4, core: 2. Of those that a mesh axis runs over, the one named last changes fastest.
Arguments:
- gradients: bfloat16 [4, 96, 1024, 1024], P('groups', None, 'shard'), may hold values from -200 to 200
- second_moment: bfloat16 [96, 1024, 1024], P('groups', 'shard'), may hold values from 0.25 to 4
- inverse_roots: bfloat16 [4, 32, 2, 2, 1024, 1024], P('groups', 'shard'), may hold values from -2 to 2
- owners: int32 [96], replicated, may hold values from 0 to 31, as said below
- weights: bfloat16 [96, 1024, 1024], P('groups', 'shard'), may hold values from -4 to 4
Outputs:
- new_weights: bfloat16 [96, 1024, 1024], P(None, 'shard')
The draws below stay inside these ranges and needn't reach their ends.
Inputs may be any that keep to these rules, and one draw needn't show every extreme that they name: `owners`: blocks 24 * g to 24 * (g + 1) - 1 form group g. Within a group no owner is named by more than 2 blocks, and some owner is named by exactly 2.
All inputs are finite; a program needn't handle non-finite values.
Results may differ from the reference program's by a relative error of at most 0.0004.
The reference program's roundings to bfloat16 on the way (of `update`) count: a program that leaves them out, or rounds other values in their place, can miss the bound.
Values may be sent and summed in bfloat16 or wider, within the bound.
No kernel may reach another device: no remote copies, remote signals or barrier semaphores. Data moves between devices by JAX's collectives and lax.ppermute only.
A program may use at most 128 MiB of HBM per device.

```python
import math
import jax
import jax.numpy as jnp
from jax import lax

BLOCK = 1024
NB = 96
NBG = 24
MOST = 2
N_GROUPS = 4
N_SHARD = 32


def draw_gradients(key, part):
    k_entries, k_row, k_col = jax.random.split(key, 3)
    row_scale = jnp.exp(jax.random.uniform(k_row, (NB, BLOCK, 1), jnp.float32, 0.0, math.log(10.0)))
    col_scale = jnp.exp(jax.random.uniform(k_col, (NB, 1, BLOCK), jnp.float32, 0.0, math.log(10.0)))
    position = jnp.arange(BLOCK, dtype=jnp.float32).reshape(1, BLOCK, 1) / BLOCK
    entries = jnp.clip(jax.random.normal(k_entries, (N_GROUPS, NB, BLOCK, BLOCK), jnp.float32), -4.0, 4.0)
    rising = jnp.exp(position * math.log(3.0))
    return (0.03 * entries * (row_scale * rising * col_scale)[None]).astype(jnp.bfloat16)


def draw_inverse_roots(key, part):
    k_diag, k_spread = jax.random.split(jax.random.fold_in(key, 11), 2)
    shape_all = (N_GROUPS, N_SHARD, MOST, 2, BLOCK, BLOCK)
    diagonal = jnp.exp(jax.random.uniform(k_diag, (N_GROUPS, N_SHARD, MOST, 2, BLOCK, 1), jnp.float32, math.log(0.5), math.log(2.0)))
    sigma = 0.5 / math.sqrt(BLOCK)
    spread_part = jnp.clip(jax.random.normal(k_spread, shape_all, jnp.float32), -4.0, 4.0) * sigma
    on_diagonal = jnp.arange(BLOCK)[:, None] == jnp.arange(BLOCK)[None, :]
    return jnp.where(on_diagonal, diagonal, spread_part).astype(jnp.bfloat16)


def draw_owners(key, part):

    def one_group(group_key):
        k_first, k_order, k_place = jax.random.split(group_key, 3)
        first_owner = jax.random.randint(k_first, (), 0, N_SHARD)
        slot_ids = jnp.arange(N_SHARD * MOST, dtype=jnp.int32)
        owner_of = slot_ids // MOST
        order_score = jax.random.permutation(k_order, N_SHARD * MOST).astype(jnp.int32)
        order_score = jnp.where(owner_of == first_owner, -1 - slot_ids % MOST, order_score)
        ranking = jnp.argsort(order_score, stable=True)
        chosen = owner_of[ranking[:NBG]]
        return chosen[jax.random.permutation(k_place, NBG)]
    group_keys = jax.random.split(jax.random.fold_in(key, 7), N_GROUPS)
    return jax.vmap(one_group)(group_keys).reshape(NB).astype(jnp.int32)


def shard_levels(own_key, dims, cuts, smallest, high):
    gain, own = 1.0, jax.random.fold_in(own_key, 6)
    for dim, parts in cuts:
        steps = jnp.exp(jax.random.uniform(jax.random.fold_in(own, dim), (parts,), jnp.float32, smallest / len(cuts), high / len(cuts)))
        gain = gain * jnp.repeat(steps, dims[dim] // parts).reshape([-1 if axis == dim else 1 for axis in range(len(dims))])
    return gain


def centred(rng, dims, width, bound, pieces=(), held_as=jnp.bfloat16):
    array = width * jax.random.normal(rng, dims, jnp.float32)
    if pieces:
        array = array * shard_levels(rng, dims, pieces, -0.22, 0.18)
    return jnp.clip(array, -bound, bound).astype(held_as)


def setup_inputs(seed: int = 0) -> dict:
    seeds = jax.random.split(jax.random.key(seed), 6)
    gradients = draw_gradients(jax.random.fold_in(seeds[5], 71), 0)
    second_moment = jnp.clip(jnp.exp(math.log(4.0) - 2.7725887 * jax.random.uniform(seeds[1], (NB, BLOCK, BLOCK), jnp.float32) ** shard_levels(seeds[1], (NB, BLOCK, BLOCK), ((0, 4), (1, 32)), -0.2, 0.2)), 0.25, 4.0).astype(jnp.bfloat16)
    inverse_roots = draw_inverse_roots(jax.random.fold_in(seeds[5], 71), 0)
    owners = draw_owners(jax.random.fold_in(seeds[5], 71), 0)
    weights = centred(seeds[4], (NB, BLOCK, BLOCK), 1.0, 4.0, ((0, 4), (1, 32)))
    return {"gradients": gradients, "second_moment": second_moment, "inverse_roots": inverse_roots, "owners": owners, "weights": weights}


def reference(gradients, second_moment, inverse_roots, owners, weights):
    total = lax.optimization_barrier(jnp.sum(gradients.astype(jnp.float32), axis=0))
    grouped = owners.reshape(N_GROUPS, NBG)
    same_owner = grouped[:, :, None] == grouped[:, None, :]
    earlier = jnp.arange(NBG)[None, :] < jnp.arange(NBG)[:, None]
    rank = lax.optimization_barrier(jnp.sum(same_owner & earlier[None], axis=2)).reshape(NB).astype(jnp.int32)
    group_ids = (jnp.arange(NB) // NBG).astype(jnp.int32)

    def update_block(items):
        block_grad, moment_old, block_weights, owner, slot, group = items
        moment = 0.95 * moment_old.astype(jnp.float32) + 0.05 * block_grad * block_grad
        adam_step = block_grad / (jnp.sqrt(moment) + 1e-08)
        graft_sq = jnp.sum(adam_step * adam_step)
        left_root = inverse_roots[group, owner, slot, 0].astype(jnp.float32)
        right_root = inverse_roots[group, owner, slot, 1].astype(jnp.float32)
        right_product = jnp.dot(block_grad, right_root, precision=lax.Precision.HIGHEST, preferred_element_type=jnp.float32)
        preconditioned = jnp.dot(left_root, right_product, precision=lax.Precision.HIGHEST, preferred_element_type=jnp.float32)
        graft_scale = jnp.sqrt(graft_sq) / jnp.sqrt(jnp.sum(preconditioned * preconditioned) + 1e-06)
        update = lax.optimization_barrier((graft_scale * preconditioned).astype(jnp.bfloat16))
        stepped = block_weights.astype(jnp.float32) - 0.5 * update.astype(jnp.float32)
        renormed = stepped * lax.rsqrt(lax.optimization_barrier(jnp.mean(stepped * stepped, axis=1, keepdims=True)) + 1e-06)
        return renormed.astype(jnp.bfloat16)
    return lax.map(update_block, (total, second_moment, weights, owners, rank, group_ids))
```

```python
import functools

import jax
import jax.numpy as jnp
from jax import lax
from jax.experimental import pallas as pl
from jax.experimental.pallas import tpu as pltpu
from jax.sharding import PartitionSpec as P


LANES = 128
CHUNKS = 2
STEP = 8
TALL = 256
ANY = pl.BlockSpec(memory_space=pl.ANY)
SMEM = pl.BlockSpec(memory_space=pltpu.SMEM)


def two_parts(values):
    high = values.astype(jnp.bfloat16)
    low = (values - high.astype(jnp.float32)).astype(jnp.bfloat16)
    return high, low


def dot(a, b):
    return jnp.dot(a, b, preferred_element_type=jnp.float32)


def sum_kernel(width, meta, own, one, two, three, old, out, norms, codes, sems):
    step = pl.program_id(0)

    def block(b, _):
        squares = jnp.zeros((1, LANES), jnp.float32)
        total = (own[0, b].astype(jnp.float32) + one[b].astype(jnp.float32)) + (
            two[b].astype(jnp.float32) + three[b].astype(jnp.float32)
        )
        moment = 0.95 * old[b].astype(jnp.float32) + 0.05 * total * total
        adam = total / (jnp.sqrt(moment) + 1e-08)
        adam = adam * adam
        parts = [total[:, j : j + LANES] for j in range(0, width, LANES)]
        top = functools.reduce(jnp.maximum, [jnp.abs(p) for p in parts])
        power = jnp.ceil(jnp.log2(jnp.maximum(top, 1e-30))) - 15.0
        grow = jnp.exp2(-power)
        at = step * STEP + b
        for j, p in enumerate(parts):
            code = jnp.clip(jnp.round(p * grow), -32767.0, 32767.0)
            codes[at, :, j * LANES : (j + 1) * LANES] = code.astype(jnp.int32).astype(jnp.int16)
            squares = squares + jnp.sum(adam[:, j * LANES : (j + 1) * LANES], axis=0, keepdims=True)
        codes[at, :, width:] = power.astype(jnp.int32).astype(jnp.int16)
        norms[at] = squares
        return 0

    lax.fori_loop(0, STEP, block, 0)

    @pl.when(step == pl.num_programs(0) - 1)
    def _():
        copies = [
            pltpu.make_async_copy(codes.at[meta[1 + n]], out.at[n], sems.at[n]) for n in range(out.shape[0])
        ]
        for c in copies:
            c.start()
        for c in copies:
            c.wait()


def sum_replicas(gradients, received, old, chunk, group, sources):
    nbg, per, width = received[0].shape
    steps = nbg // STEP
    count = sources.shape[0]
    part = pl.BlockSpec((STEP, per, width), lambda i, meta: (i, 0, 0))
    return pl.pallas_call(
        functools.partial(sum_kernel, width),
        out_shape=(
            jax.ShapeDtypeStruct((count, per, width + LANES), jnp.int16),
            jax.ShapeDtypeStruct((nbg, 1, LANES), jnp.float32),
        ),
        grid_spec=pltpu.PrefetchScalarGridSpec(
            num_scalar_prefetch=1,
            grid=(steps,),
            in_specs=[
                pl.BlockSpec((1, STEP, per, width), lambda i, meta: (0, meta[0] * steps + i, chunk, 0)),
                part,
                part,
                part,
                pl.BlockSpec((STEP, per, width), lambda i, meta: (i, chunk, 0)),
            ],
            out_specs=[ANY, pl.BlockSpec((nbg, 1, LANES), lambda i, meta: (0, 0, 0))],
            scratch_shapes=[
                pltpu.VMEM((nbg, per, width + LANES), jnp.int16),
                pltpu.SemaphoreType.DMA((count,)),
            ],
        ),
    )(jnp.concatenate([group[None].astype(jnp.int32), sources]), gradients, *received, old)


def owner_kernel(width, graft, roots, *refs):
    arrived, update, high, low, pre = refs[:-4], refs[-4], refs[-3], refs[-2], refs[-1]
    n_src = arrived[0].shape[0]
    per = arrived[0].shape[-2]
    rows = per * len(arrived)

    def unpack(n, _):
        for c, code in enumerate(arrived):
            at = pl.ds(pl.multiple_of(n * rows + c * per, per), per)
            got = code[n, 0] if len(code.shape) == 4 else code[n]
            step = jnp.exp2(got[:, width:].astype(jnp.int32).astype(jnp.float32))
            for j in range(0, width, LANES):
                value = got[:, j : j + LANES].astype(jnp.int32).astype(jnp.float32) * step
                high[at, j : j + LANES], low[at, j : j + LANES] = two_parts(value)
        return 0

    lax.fori_loop(0, n_src, unpack, 0)
    right = roots[0, 0, 0, 1]
    for m in range(0, width, TALL):
        at = pl.ds(m, TALL)
        high[at, :], low[at, :] = two_parts(dot(high[at, :], right) + dot(low[at, :], right))
    square = jnp.zeros((1, width), jnp.float32)
    for m in range(0, width, TALL):
        at = pl.ds(m, TALL)
        left = roots[0, 0, 0, 0, at, :]
        got = dot(left, high[...]) + dot(left, low[...])
        pre[at, :] = got
        square = square + jnp.sum(got * got, axis=0, keepdims=True)
    square = jnp.sum(square, axis=1, keepdims=True)
    scale = jnp.sqrt(jnp.full((1, 1), graft[0], jnp.float32)) / jnp.sqrt(square + 1e-06)
    for m in range(0, width, TALL):
        at = pl.ds(m, TALL)
        update[at, :] = (scale * pre[at, :]).astype(jnp.bfloat16)


def owner_work(graft, roots, arrived, slot):
    width = roots.shape[-1]
    specs = []
    for a in arrived:
        if a.ndim == 4:
            specs.append(pl.BlockSpec((a.shape[0], 1) + a.shape[2:], lambda i: (0, slot, 0, 0)))
        else:
            specs.append(pl.BlockSpec(a.shape, lambda i: (0, 0, 0)))
    return pl.pallas_call(
        functools.partial(owner_kernel, width),
        out_shape=jax.ShapeDtypeStruct((width, width), jnp.bfloat16),
        grid=(1,),
        in_specs=[SMEM, pl.BlockSpec((1, 1, 1, 2, width, width), lambda i: (0, 0, slot, 0, 0, 0))] + specs,
        out_specs=pl.BlockSpec((width, width), lambda i: (0, 0)),
        scratch_shapes=[
            pltpu.VMEM((width, width), jnp.bfloat16),
            pltpu.VMEM((width, width), jnp.bfloat16),
            pltpu.VMEM((width, width), jnp.float32),
        ],
    )(graft.reshape(1), roots, *arrived)


def renew_kernel(count, table, weights, *refs):
    backs, outs, held, grads, sems = refs[:-5], refs[-5:-3], refs[-3], refs[-2], refs[-1]

    def fetch(j):
        return pltpu.make_async_copy(weights.at[table[j]], held.at[j], sems.at[0, j])

    def pull(j, k):
        return pltpu.make_async_copy(backs[k].at[table[count + j]], grads.at[j], sems.at[1, j])

    for j in range(count):
        fetch(j).start()
        if len(backs) == 1:
            pull(j, 0).start()
        else:
            for k in range(len(backs)):

                @pl.when(table[2 * count + j] == k)
                def _():
                    pull(j, k).start()

    half = count // 2
    for j in range(count):
        fetch(j).wait()
        pull(j, 0).wait()
        stepped = held[j].astype(jnp.float32) - 0.5 * grads[j].astype(jnp.float32)
        scale = lax.rsqrt(jnp.mean(stepped * stepped, axis=1, keepdims=True) + 1e-06)
        outs[j // half][j % half] = (stepped * scale).astype(jnp.bfloat16)


def renew(table, weights, backs):
    count = table.shape[0] // 3
    rows, width = weights.shape[1:]
    half = jax.ShapeDtypeStruct((count // 2, rows, width), jnp.bfloat16)
    return pl.pallas_call(
        functools.partial(renew_kernel, count),
        out_shape=(half, half),
        in_specs=[SMEM] + [ANY] * (1 + len(backs)),
        scratch_shapes=[
            pltpu.VMEM((count, rows, width), jnp.bfloat16),
            pltpu.VMEM((count, rows, width), jnp.bfloat16),
            pltpu.SemaphoreType.DMA((2, count)),
        ],
    )(table, weights, *backs)


def scatter_kernel(place, *refs):
    pieces, out, sems = refs[:-2], refs[-2], refs[-1]
    copies = []
    for piece in pieces:
        for j in range(piece.shape[0]):
            n = len(copies)
            copies.append(pltpu.make_async_copy(piece.at[j], out.at[place[n]], sems.at[n]))
    for c in copies:
        c.start()
    for c in copies:
        c.wait()


def scatter_more_kernel(place, base, *refs):
    del base
    scatter_kernel(place, *refs)


def scatter_blocks(place, pieces, out_shape, base=None):
    count = sum(p.shape[0] for p in pieces)
    operands = list(pieces) if base is None else [base] + list(pieces)
    return pl.pallas_call(
        scatter_kernel if base is None else scatter_more_kernel,
        out_shape=out_shape,
        in_specs=[SMEM] + [ANY] * len(operands),
        out_specs=ANY,
        scratch_shapes=[pltpu.SemaphoreType.DMA((count,))],
        input_output_aliases={} if base is None else {1: 0},
    )(place, *operands)


def body(gradients, second_moment, inverse_roots, owners, weights):
    groups = lax.axis_size("groups")
    shards = lax.axis_size("shard")
    g = lax.axis_index("groups")
    s = lax.axis_index("shard")
    total_blocks = owners.shape[0]
    nbg = total_blocks // groups
    slots = inverse_roots.shape[2]
    rows = gradients.shape[2]
    width = gradients.shape[3]
    half = nbg // 2

    def shift(n):
        return [(i, (i + n) % groups) for i in range(groups)]

    per = rows // CHUNKS
    received = []
    grads = gradients
    for c in range(CHUNKS):
        pieces = [
            lax.dynamic_slice(grads[0], (nbg * ((g + n) % groups), c * per, 0), (nbg, per, width)) for n in (1, 3, 2)
        ]
        grads, pieces = lax.optimization_barrier((grads, pieces))
        received.append([lax.ppermute(p, "groups", shift(n)) for p, n in zip(pieces, (1, 3, 2))])

    grouped = owners.reshape(groups, nbg)
    same = grouped[:, :, None] == grouped[:, None, :]
    ids = jnp.arange(nbg, dtype=jnp.int32)
    earlier = ids[None, :] < ids[:, None]
    rank = jnp.sum((same & earlier[None]).astype(jnp.int32), axis=2)
    firsts = rank == 0
    before = jnp.sum((firsts[:, None, :] & earlier[None]).astype(jnp.int32), axis=2)
    n_first = jnp.sum(firsts.astype(jnp.int32), axis=1, keepdims=True)
    spot = jnp.where(firsts, before, n_first + ids[None] - before)
    sits = spot[:, None, :] == ids[None, :, None]
    order = jnp.sum(jnp.where(sits, ids[None, None, :], 0), axis=2)
    by_order = [
        lax.dynamic_index_in_dim(jnp.sum(jnp.where(sits, t[:, None, :], 0), axis=2), g, 0, False)
        for t in (jnp.broadcast_to(ids[None], grouped.shape), grouped, rank)
    ]
    my_owner = lax.dynamic_index_in_dim(grouped, g, 0, False)
    my_rank = lax.dynamic_index_in_dim(rank, g, 0, False)
    dest = jnp.arange(shards, dtype=jnp.int32)
    match = [(my_owner[None, :] == dest[:, None]) & (my_rank[None, :] == k) for k in range(slots)]
    source = [jnp.sum(jnp.where(m, ids[None], 0), axis=1) for m in match]
    mine = [(my_owner == s) & (my_rank == k) for k in range(slots)]

    codes, norms = [], []
    for c in range(CHUNKS):
        if c < CHUNKS - 1:
            wanted = jnp.stack(source, 1).reshape(-1)
        else:
            wanted = jnp.concatenate(source)
        code, norm = sum_replicas(gradients, received[c], second_moment, c, g, wanted)
        codes.append(code)
        norms.append(norm)
    arrived = [[] for _ in range(slots)]
    for c in range(CHUNKS - 1):
        got = lax.all_to_all(codes[c].reshape(shards, slots, per, width + LANES), "shard", 0, 0, tiled=True)
        for k in range(slots):
            arrived[k].append(got)
    for k in range(slots):
        arrived[k].append(lax.all_to_all(codes[-1][k * shards : (k + 1) * shards], "shard", 0, 0, tiled=True))

    partial = sum(jnp.sum(n, axis=(1, 2)) for n in norms)
    n = 1
    while n < shards:
        partial = partial + lax.ppermute(partial, "shard", [(i, i ^ n) for i in range(shards)])
        n *= 2
    graft = [jnp.sum(jnp.where(m, partial, 0.0)) for m in mine]

    backs = []
    for k in range(slots):
        update = owner_work(graft[k], inverse_roots, arrived[k], k)
        backs.append(lax.all_to_all(update.reshape(shards, rows, width), "shard", 0, 0, tiled=True))

    def to_all(new):
        a, b = new
        prev_a = lax.ppermute(a, "groups", shift(1))
        after_b = lax.ppermute(b, "groups", shift(3))
        prev_b = lax.ppermute(b, "groups", shift(1))
        after_a = lax.ppermute(a, "groups", shift(3))
        far_a = lax.ppermute(prev_a, "groups", shift(1))
        far_b = lax.ppermute(after_b, "groups", shift(3))
        return [a, b, prev_a, prev_b, after_a, after_b, far_a, far_b]

    def places(lo, hi):
        out = []
        for n in (0, 3, 1, 2):
            h = (g + n) % groups
            out.append(nbg * h + lax.dynamic_index_in_dim(order, h, 0, False)[lo:hi])
        return jnp.concatenate(out)

    def table(lo, hi):
        return jnp.concatenate([t[lo:hi] for t in by_order])

    out_shape = jax.ShapeDtypeStruct((total_blocks, rows, width), jnp.bfloat16)
    first = to_all(renew(table(0, half), weights, backs[:1]))
    second = to_all(renew(table(half, nbg), weights, backs))
    out = scatter_blocks(places(0, half), first, out_shape)
    return scatter_blocks(places(half, nbg), second, out_shape, base=out)


def solution(mesh):
    return jax.shard_map(
        body,
        mesh=mesh,
        in_specs=(
            P("groups", None, "shard", None),
            P("groups", "shard", None),
            P("groups", "shard", None, None, None, None),
            P(),
            P("groups", "shard", None),
        ),
        out_specs=P(None, "shard", None),
        check_vma=False,
    )
```

```python
import functools

import jax
import jax.numpy as jnp
from jax import lax
from jax.experimental import pallas as pl
from jax.experimental.pallas import tpu as pltpu
from jax.sharding import PartitionSpec as P


LANES = 128
CHUNKS = 2
STEP = 8
TALL = 256
ANY = pl.BlockSpec(memory_space=pl.ANY)
SMEM = pl.BlockSpec(memory_space=pltpu.SMEM)


def two_parts(values):
    high = values.astype(jnp.bfloat16)
    low = (values - high.astype(jnp.float32)).astype(jnp.bfloat16)
    return high, low


def dot(a, b):
    return jnp.dot(a, b, preferred_element_type=jnp.float32)


def sum_kernel(width, last, meta, own, one, two, three, old, *refs):
    before = refs[0] if last else None
    outs = refs[1 if last else 0 : -2]
    norms = None if last else outs[-1]
    outs = outs if last else outs[:-1]
    codes, sems = refs[-2:]
    step = pl.program_id(0)

    def block(b, _):
        total = (own[0, b].astype(jnp.float32) + one[b].astype(jnp.float32)) + (
            two[b].astype(jnp.float32) + three[b].astype(jnp.float32)
        )
        moment = 0.95 * old[b].astype(jnp.float32) + 0.05 * total * total
        adam = total / (jnp.sqrt(moment) + 1e-08)
        adam = adam * adam
        parts = [total[:, j : j + LANES] for j in range(0, width, LANES)]
        top = functools.reduce(jnp.maximum, [jnp.abs(p) for p in parts])
        power = jnp.ceil(jnp.log2(jnp.maximum(top, 1e-30))) - 15.0
        grow = jnp.exp2(-power)
        at = step * STEP + b
        for j, p in enumerate(parts):
            code = jnp.clip(jnp.round(p * grow), -32767.0, 32767.0)
            codes[at, :, j * LANES : (j + 1) * LANES] = code.astype(jnp.int32).astype(jnp.int16)
        codes[at, :, width : width + LANES] = power.astype(jnp.int32).astype(jnp.int16)
        squares = functools.reduce(jnp.add, [adam[:, j : j + LANES] for j in range(0, width, LANES)])
        squares = jnp.sum(squares, axis=0, keepdims=True)
        if not last:
            norms[at] = squares
            return 0
        squares = squares + before[at]
        power = jnp.ceil(jnp.log2(jnp.maximum(squares, 1e-30)))
        scaled = squares * jnp.exp2(14.0 - power)
        high = jnp.floor(scaled)
        low = jnp.floor((scaled - high) * 16384.0)
        row = lax.broadcasted_iota(jnp.int32, (codes.shape[1], LANES), 0)
        full = jnp.where(row == 0, power, jnp.where(row == 1, high, low))
        codes[at, :, width + LANES :] = full.astype(jnp.int32).astype(jnp.int16)
        return 0

    lax.fori_loop(0, STEP, block, 0)

    @pl.when(step == pl.num_programs(0) - 1)
    def _():
        copies = []
        for out in outs:
            for n in range(out.shape[0]):
                k = len(copies)
                copies.append(pltpu.make_async_copy(codes.at[meta[1 + k]], out.at[n], sems.at[k]))
        for c in copies:
            c.start()
        for c in copies:
            c.wait()


def sum_replicas(gradients, received, old, chunk, group, sources, before=None):
    nbg, per, width = received[0].shape
    steps = nbg // STEP
    last = before is not None
    columns = width + (2 if last else 1) * LANES
    count = sum(x.shape[0] for x in sources)
    part = pl.BlockSpec((STEP, per, width), lambda i, meta: (i, 0, 0))
    whole = pl.BlockSpec((nbg, 1, LANES), lambda i, meta: (0, 0, 0))
    shapes = [jax.ShapeDtypeStruct((x.shape[0], per, columns), jnp.int16) for x in sources]
    if not last:
        shapes.append(jax.ShapeDtypeStruct((nbg, 1, LANES), jnp.float32))
    return pl.pallas_call(
        functools.partial(sum_kernel, width, last),
        out_shape=shapes,
        grid_spec=pltpu.PrefetchScalarGridSpec(
            num_scalar_prefetch=1,
            grid=(steps,),
            in_specs=[
                pl.BlockSpec((1, STEP, per, width), lambda i, meta: (0, meta[0] * steps + i, chunk, 0)),
                part,
                part,
                part,
                pl.BlockSpec((STEP, per, width), lambda i, meta: (i, chunk, 0)),
            ]
            + ([whole] if last else []),
            out_specs=[ANY] * len(sources) + ([] if last else [whole]),
            scratch_shapes=[
                pltpu.VMEM((nbg, per, columns), jnp.int16),
                pltpu.SemaphoreType.DMA((count,)),
            ],
        ),
    )(
        jnp.concatenate([group[None].astype(jnp.int32), *sources]),
        gradients,
        *received,
        old,
        *([before] if last else []),
    )


def owner_kernel(width, roots, *refs):
    arrived, update, high, low, pre = refs[:-4], refs[-4], refs[-3], refs[-2], refs[-1]
    n_src = arrived[0].shape[0]
    per = arrived[0].shape[-2]
    rows = per * len(arrived)

    def unpack(n, graft):
        for c, code in enumerate(arrived):
            at = pl.ds(pl.multiple_of(n * rows + c * per, per), per)
            got = code[n, 0] if len(code.shape) == 4 else code[n]
            step = jnp.exp2(got[:, width : width + LANES].astype(jnp.int32).astype(jnp.float32))
            for j in range(0, width, LANES):
                value = got[:, j : j + LANES].astype(jnp.int32).astype(jnp.float32) * step
                high[at, j : j + LANES], low[at, j : j + LANES] = two_parts(value)
        norm = got[:, width + LANES :].astype(jnp.int32).astype(jnp.float32)
        return graft + jnp.exp2(norm[0:1] - 14.0) * (norm[1:2] + norm[2:3] * (1.0 / 16384.0))

    graft = lax.fori_loop(0, n_src, unpack, jnp.zeros((1, LANES), jnp.float32))
    graft = jnp.sum(graft, axis=1, keepdims=True)
    right = roots[0, 0, 0, 1]
    for m in range(0, width, TALL):
        at = pl.ds(m, TALL)
        high[at, :], low[at, :] = two_parts(dot(high[at, :], right) + dot(low[at, :], right))
    square = jnp.zeros((1, width), jnp.float32)
    for m in range(0, width, TALL):
        at = pl.ds(m, TALL)
        left = roots[0, 0, 0, 0, at, :]
        got = dot(left, high[...]) + dot(left, low[...])
        pre[at, :] = got
        square = square + jnp.sum(got * got, axis=0, keepdims=True)
    square = jnp.sum(square, axis=1, keepdims=True)
    scale = jnp.sqrt(graft) / jnp.sqrt(square + 1e-06)
    for m in range(0, width, TALL):
        at = pl.ds(m, TALL)
        update[at, :] = (scale * pre[at, :]).astype(jnp.bfloat16)


def owner_work(roots, arrived, slot):
    width = roots.shape[-1]
    specs = []
    for a in arrived:
        if a.ndim == 4:
            specs.append(pl.BlockSpec((a.shape[0], 1) + a.shape[2:], lambda i: (0, slot, 0, 0)))
        else:
            specs.append(pl.BlockSpec(a.shape, lambda i: (0, 0, 0)))
    return pl.pallas_call(
        functools.partial(owner_kernel, width),
        out_shape=jax.ShapeDtypeStruct((width, width), jnp.bfloat16),
        grid=(1,),
        in_specs=[pl.BlockSpec((1, 1, 1, 2, width, width), lambda i: (0, 0, slot, 0, 0, 0))] + specs,
        out_specs=pl.BlockSpec((width, width), lambda i: (0, 0)),
        scratch_shapes=[
            pltpu.VMEM((width, width), jnp.bfloat16),
            pltpu.VMEM((width, width), jnp.bfloat16),
            pltpu.VMEM((width, width), jnp.float32),
        ],
    )(roots, *arrived)


def renew_kernel(count, table, weights, *refs):
    backs, outs, held, grads, sems = refs[:-5], refs[-5:-3], refs[-3], refs[-2], refs[-1]

    def fetch(j):
        return pltpu.make_async_copy(weights.at[table[j]], held.at[j], sems.at[0, j])

    def pull(j, k):
        return pltpu.make_async_copy(backs[k].at[table[count + j]], grads.at[j], sems.at[1, j])

    for j in range(count):
        fetch(j).start()
        if len(backs) == 1:
            pull(j, 0).start()
        else:
            for k in range(len(backs)):

                @pl.when(table[2 * count + j] == k)
                def _():
                    pull(j, k).start()

    half = count // 2
    for j in range(count):
        fetch(j).wait()
        pull(j, 0).wait()
        stepped = held[j].astype(jnp.float32) - 0.5 * grads[j].astype(jnp.float32)
        scale = lax.rsqrt(jnp.mean(stepped * stepped, axis=1, keepdims=True) + 1e-06)
        outs[j // half][j % half] = (stepped * scale).astype(jnp.bfloat16)


def renew(table, weights, backs):
    count = table.shape[0] // 3
    rows, width = weights.shape[1:]
    half = jax.ShapeDtypeStruct((count // 2, rows, width), jnp.bfloat16)
    return pl.pallas_call(
        functools.partial(renew_kernel, count),
        out_shape=(half, half),
        in_specs=[SMEM] + [ANY] * (1 + len(backs)),
        scratch_shapes=[
            pltpu.VMEM((count, rows, width), jnp.bfloat16),
            pltpu.VMEM((count, rows, width), jnp.bfloat16),
            pltpu.SemaphoreType.DMA((2, count)),
        ],
    )(table, weights, *backs)


def pass_kernel(table, *refs):
    for j in range(table.shape[0]):
        refs[-1][j] = table[j]


def pass_table(table, *after):
    return pl.pallas_call(
        pass_kernel,
        out_shape=jax.ShapeDtypeStruct(table.shape, table.dtype),
        in_specs=[SMEM] + [ANY] * len(after),
        out_specs=SMEM,
    )(table, *after)


def scatter_kernel(place, *refs):
    pieces, out, sems = refs[:-2], refs[-2], refs[-1]
    copies = []
    for piece in pieces:
        for j in range(piece.shape[0]):
            n = len(copies)
            copies.append(pltpu.make_async_copy(piece.at[j], out.at[place[n]], sems.at[n]))
    for c in copies:
        c.start()
    for c in copies:
        c.wait()


def scatter_more_kernel(place, base, *refs):
    del base
    scatter_kernel(place, *refs)


def scatter_blocks(place, pieces, out_shape, base=None):
    count = sum(p.shape[0] for p in pieces)
    operands = list(pieces) if base is None else [base] + list(pieces)
    return pl.pallas_call(
        scatter_kernel if base is None else scatter_more_kernel,
        out_shape=out_shape,
        in_specs=[SMEM] + [ANY] * (len(operands) - len(pieces)) + [pl.BlockSpec(memory_space=pltpu.VMEM)] * len(pieces),
        out_specs=ANY,
        scratch_shapes=[pltpu.SemaphoreType.DMA((count,))],
        input_output_aliases={} if base is None else {1: 0},
    )(place, *operands)


def body(gradients, second_moment, inverse_roots, owners, weights):
    groups = lax.axis_size("groups")
    shards = lax.axis_size("shard")
    g = lax.axis_index("groups")
    total_blocks = owners.shape[0]
    nbg = total_blocks // groups
    slots = inverse_roots.shape[2]
    rows = gradients.shape[2]
    width = gradients.shape[3]
    half = nbg // 2

    def shift(n):
        return [(i, (i + n) % groups) for i in range(groups)]

    per = rows // CHUNKS
    received = []
    grads = gradients
    for c in range(CHUNKS):
        pieces = [
            lax.dynamic_slice(grads[0], (nbg * ((g + n) % groups), c * per, 0), (nbg, per, width)) for n in (1, 3, 2)
        ]
        grads, pieces = lax.optimization_barrier((grads, pieces))
        received.append([lax.ppermute(p, "groups", shift(n)) for p, n in zip(pieces, (1, 3, 2))])

    grouped = owners.reshape(groups, nbg)
    same = grouped[:, :, None] == grouped[:, None, :]
    ids = jnp.arange(nbg, dtype=jnp.int32)
    earlier = ids[None, :] < ids[:, None]
    rank = jnp.sum((same & earlier[None]).astype(jnp.int32), axis=2)
    firsts = rank == 0
    before = jnp.sum((firsts[:, None, :] & earlier[None]).astype(jnp.int32), axis=2)
    n_first = jnp.sum(firsts.astype(jnp.int32), axis=1, keepdims=True)
    spot = jnp.where(firsts, before, n_first + ids[None] - before)
    sits = spot[:, None, :] == ids[None, :, None]
    order = jnp.sum(jnp.where(sits, ids[None, None, :], 0), axis=2)
    by_order = [
        lax.dynamic_index_in_dim(jnp.sum(jnp.where(sits, t[:, None, :], 0), axis=2), g, 0, False)
        for t in (jnp.broadcast_to(ids[None], grouped.shape), grouped, rank)
    ]
    my_owner = lax.dynamic_index_in_dim(grouped, g, 0, False)
    my_rank = lax.dynamic_index_in_dim(rank, g, 0, False)
    dest = jnp.arange(shards, dtype=jnp.int32)
    match = [(my_owner[None, :] == dest[:, None]) & (my_rank[None, :] == k) for k in range(slots)]
    source = [jnp.sum(jnp.where(m, ids[None], 0), axis=1) for m in match]

    def exchange(x, after=None):
        if after is not None:
            x, after = lax.optimization_barrier((x, after))
        return lax.all_to_all(x, "shard", 0, 0, tiled=True)

    code, norm = sum_replicas(gradients, received[0], second_moment, 0, g, [jnp.stack(source, 1).reshape(-1)])
    codes = sum_replicas(gradients, received[1], second_moment, 1, g, source, norm)
    first = exchange(code.reshape(shards, slots, per, width + LANES))
    arrived = []
    for k in range(slots):
        arrived.append([first, exchange(codes[k], arrived[-1][-1] if k else first)])

    backs = []
    for k in range(slots):
        update = owner_work(inverse_roots, arrived[k], k)
        backs.append(exchange(update.reshape(shards, rows, width), backs[-1] if k else None))

    def to_all(new):
        a, b = new
        prev_a = lax.ppermute(a, "groups", shift(1))
        after_b = lax.ppermute(b, "groups", shift(3))
        prev_b = lax.ppermute(b, "groups", shift(1))
        after_a = lax.ppermute(a, "groups", shift(3))
        far_a = lax.ppermute(prev_a, "groups", shift(1))
        far_b = lax.ppermute(after_b, "groups", shift(3))
        return [a, b, prev_a, prev_b, after_a, after_b, far_a, far_b]

    def places(lo, hi):
        out = []
        for n in (0, 3, 1, 2):
            h = (g + n) % groups
            out.append(nbg * h + lax.dynamic_index_in_dim(order, h, 0, False)[lo:hi])
        return jnp.concatenate(out)

    def table(lo, hi):
        return jnp.concatenate([t[lo:hi] for t in by_order])

    out_shape = jax.ShapeDtypeStruct((total_blocks, rows, width), jnp.bfloat16)
    new = renew(table(0, half), weights, backs[:1])
    pieces0 = to_all(new)
    late = pass_table(table(half, nbg), pieces0[2], pieces0[5])
    new = renew(late, weights, backs)
    pieces1 = to_all(new)
    out = scatter_blocks(places(0, half), pieces0, out_shape)
    return scatter_blocks(places(half, nbg), pieces1, out_shape, base=out)


def solution(mesh):
    return jax.shard_map(
        body,
        mesh=mesh,
        in_specs=(
            P("groups", None, "shard", None),
            P("groups", "shard", None),
            P("groups", "shard", None, None, None, None),
            P(),
            P("groups", "shard", None),
        ),
        out_specs=P(None, "shard", None),
        check_vma=False,
    )
```

```python
import functools

import jax
import jax.numpy as jnp
from jax import lax
from jax.experimental import pallas as pl
from jax.experimental.pallas import tpu as pltpu
from jax.sharding import PartitionSpec as P


LANES = 128
CHUNKS = (8, 8, 16)
STEP = 8
TALL = 256
ANY = pl.BlockSpec(memory_space=pl.ANY)
SMEM = pl.BlockSpec(memory_space=pltpu.SMEM)


def two_parts(values):
    high = values.astype(jnp.bfloat16)
    low = (values - high.astype(jnp.float32)).astype(jnp.bfloat16)
    return high, low


def dot(a, b):
    return jnp.dot(a, b, preferred_element_type=jnp.float32)


def sum_kernel(width, first, last, meta, own, one, two, three, old, *refs):
    before = None if first else refs[0]
    outs = refs[0 if first else 1 : -2]
    norms = None if last else outs[-1]
    outs = outs if last else outs[:-1]
    codes, sems = refs[-2:]
    step = pl.program_id(0)

    def block(b, _):
        total = (own[0, b].astype(jnp.float32) + one[b].astype(jnp.float32)) + (
            two[b].astype(jnp.float32) + three[b].astype(jnp.float32)
        )
        moment = 0.95 * old[b].astype(jnp.float32) + 0.05 * total * total
        adam = total / (moment * lax.rsqrt(moment) + 1e-08)
        adam = adam * adam
        parts = [total[:, j : j + LANES] for j in range(0, width, LANES)]
        top = functools.reduce(jnp.maximum, [jnp.abs(p) for p in parts])
        if last:
            top = jnp.maximum(top[:8], top[8:])
        power = jnp.floor(jnp.log2(jnp.maximum(top, 1e-30)) + 1e-4) - 14.0
        grow = jnp.exp2(-power)
        if last:
            grow = jnp.concatenate([grow, grow], axis=0)
        at = step * STEP + b
        for j, p in enumerate(parts):
            codes[at, :, j * LANES : (j + 1) * LANES] = jnp.round(p * grow).astype(jnp.int32).astype(jnp.int16)
        squares = functools.reduce(jnp.add, [adam[:, j : j + LANES] for j in range(0, width, LANES)])
        squares = jnp.sum(squares, axis=0, keepdims=True)
        if not first:
            squares = squares + before[at]
        if not last:
            norms[at] = squares
            codes[at, :, width:] = power.astype(jnp.int32).astype(jnp.int16)
            return 0
        scale = jnp.ceil(jnp.log2(jnp.maximum(squares, 1e-30)))
        scaled = squares * jnp.exp2(14.0 - scale)
        high = jnp.floor(scaled)
        low = jnp.floor((scaled - high) * 16384.0)
        row = lax.broadcasted_iota(jnp.int32, (8, LANES), 0)
        full = jnp.where(row == 0, scale, jnp.where(row == 1, high, low))
        full = jnp.concatenate([power, full], axis=0)
        codes[at, :, width:] = full.astype(jnp.int32).astype(jnp.int16)
        return 0

    lax.fori_loop(0, STEP, block, 0)

    @pl.when(step == pl.num_programs(0) - 1)
    def _():
        copies = []
        for out in outs:
            for n in range(out.shape[0]):
                k = len(copies)
                copies.append(pltpu.make_async_copy(codes.at[meta[1 + k]], out.at[n], sems.at[k]))
        for c in copies:
            c.start()
        for c in copies:
            c.wait()


def sum_replicas(gradients, received, old, start, group, sources, before, last):
    nbg, per, width = received[0].shape
    steps = nbg // STEP
    chunk = start // per
    columns = width + LANES
    count = sum(x.shape[0] for x in sources)
    part = pl.BlockSpec((STEP, per, width), lambda i, meta: (i, 0, 0))
    whole = pl.BlockSpec((nbg, 1, LANES), lambda i, meta: (0, 0, 0))
    shapes = [jax.ShapeDtypeStruct((x.shape[0], per, columns), jnp.int16) for x in sources]
    if not last:
        shapes.append(jax.ShapeDtypeStruct((nbg, 1, LANES), jnp.float32))
    carried = [] if before is None else [before]
    return pl.pallas_call(
        functools.partial(sum_kernel, width, before is None, last),
        out_shape=shapes,
        grid_spec=pltpu.PrefetchScalarGridSpec(
            num_scalar_prefetch=1,
            grid=(steps,),
            in_specs=[
                pl.BlockSpec((1, STEP, per, width), lambda i, meta: (0, meta[0] * steps + i, chunk, 0)),
                part,
                part,
                part,
                pl.BlockSpec((STEP, per, width), lambda i, meta: (i, chunk, 0)),
            ]
            + [whole] * len(carried),
            out_specs=[ANY] * len(sources) + ([] if last else [whole]),
            scratch_shapes=[
                pltpu.VMEM((nbg, per, columns), jnp.int16),
                pltpu.SemaphoreType.DMA((count,)),
            ],
        ),
    )(jnp.concatenate([group[None].astype(jnp.int32), *sources]), gradients, *received, old, *carried)


def owner_kernel(width, roots, *refs):
    arrived, update, high, low, pre = refs[:-4], refs[-4], refs[-3], refs[-2], refs[-1]
    n_src = arrived[0].shape[0]
    early, final = arrived[:-1], arrived[-1]
    top = sum(a.shape[-2] for a in early)
    rows = top + final.shape[-2]

    def step_of(powers):
        return jnp.exp2(powers.astype(jnp.int32).astype(jnp.float32))

    def unpack(n, graft):
        at = pl.ds(pl.multiple_of(n * rows, rows), top)
        got = [a[n, 0] for a in early]
        steps = [step_of(x[:, width:]) for x in got]
        for j in range(0, width, LANES):
            value = [x[:, j : j + LANES].astype(jnp.int32).astype(jnp.float32) * t for x, t in zip(got, steps)]
            high[at, j : j + LANES], low[at, j : j + LANES] = two_parts(jnp.concatenate(value, axis=0))
        at = pl.ds(pl.multiple_of(n * rows + top, top), rows - top)
        got = final[n]
        tail = got[:, width:].astype(jnp.int32).astype(jnp.float32)
        step = jnp.exp2(tail[:8])
        step = jnp.concatenate([step, step], axis=0)
        for j in range(0, width, LANES):
            value = got[:, j : j + LANES].astype(jnp.int32).astype(jnp.float32) * step
            high[at, j : j + LANES], low[at, j : j + LANES] = two_parts(value)
        return graft + jnp.exp2(tail[8:9] - 14.0) * (tail[9:10] + tail[10:11] * (1.0 / 16384.0))

    graft = lax.fori_loop(0, n_src, unpack, jnp.zeros((1, LANES), jnp.float32))
    graft = jnp.sum(graft, axis=1, keepdims=True)
    right = roots[0, 0, 0, 1]
    for m in range(0, width, TALL):
        at = pl.ds(m, TALL)
        high[at, :], low[at, :] = two_parts(dot(high[at, :], right) + dot(low[at, :], right))
    square = jnp.zeros((1, width), jnp.float32)
    for m in range(0, width, TALL):
        at = pl.ds(m, TALL)
        left = roots[0, 0, 0, 0, at, :]
        got = dot(left, high[...]) + dot(left, low[...])
        pre[at, :] = got
        square = square + jnp.sum(got * got, axis=0, keepdims=True)
    square = jnp.sum(square, axis=1, keepdims=True)
    scale = jnp.sqrt(graft) / jnp.sqrt(square + 1e-06)
    for m in range(0, width, TALL):
        at = pl.ds(m, TALL)
        update[at, :] = (scale * pre[at, :]).astype(jnp.bfloat16)


def owner_work(roots, arrived, slot):
    width = roots.shape[-1]
    specs = []
    for a in arrived:
        if a.ndim == 4:
            specs.append(pl.BlockSpec((a.shape[0], 1) + a.shape[2:], lambda i: (0, slot, 0, 0)))
        else:
            specs.append(pl.BlockSpec(a.shape, lambda i: (0, 0, 0)))
    return pl.pallas_call(
        functools.partial(owner_kernel, width),
        out_shape=jax.ShapeDtypeStruct((width, width), jnp.bfloat16),
        grid=(1,),
        in_specs=[pl.BlockSpec((1, 1, 1, 2, width, width), lambda i: (0, 0, slot, 0, 0, 0))] + specs,
        out_specs=pl.BlockSpec((width, width), lambda i: (0, 0)),
        scratch_shapes=[
            pltpu.VMEM((width, width), jnp.bfloat16),
            pltpu.VMEM((width, width), jnp.bfloat16),
            pltpu.VMEM((width, width), jnp.float32),
        ],
    )(roots, *arrived)


def renew_kernel(count, table, weights, *refs):
    backs, outs, held, sems = refs[:-4], refs[-4:-2], refs[-2], refs[-1]
    copies = [pltpu.make_async_copy(weights.at[table[j]], held.at[j], sems.at[j]) for j in range(count)]
    for c in copies:
        c.start()
    half = count // 2
    for j in range(count):
        grad = backs[0][table[count + j]].astype(jnp.float32)
        for k in range(1, len(backs)):
            grad = jnp.where(table[2 * count + j] == k, backs[k][table[count + j]].astype(jnp.float32), grad)
        copies[j].wait()
        stepped = held[j].astype(jnp.float32) - 0.5 * grad
        scale = lax.rsqrt(jnp.mean(stepped * stepped, axis=1, keepdims=True) + 1e-06)
        outs[j // half][j % half] = (stepped * scale).astype(jnp.bfloat16)


def renew(table, weights, backs):
    count = table.shape[0] // 3
    rows, width = weights.shape[1:]
    half = jax.ShapeDtypeStruct((count // 2, rows, width), jnp.bfloat16)
    return pl.pallas_call(
        functools.partial(renew_kernel, count),
        out_shape=(half, half),
        in_specs=[SMEM, ANY] + [pl.BlockSpec(memory_space=pltpu.VMEM)] * len(backs),
        scratch_shapes=[
            pltpu.VMEM((count, rows, width), jnp.bfloat16),
            pltpu.SemaphoreType.DMA((count,)),
        ],
    )(table, weights, *backs)


def pass_kernel(table, *refs):
    for j in range(table.shape[0]):
        refs[-1][j] = table[j]


def pass_table(table, *after):
    return pl.pallas_call(
        pass_kernel,
        out_shape=jax.ShapeDtypeStruct(table.shape, table.dtype),
        in_specs=[SMEM] + [ANY] * len(after),
        out_specs=SMEM,
    )(table, *after)


def scatter_kernel(place, *refs):
    pieces, out, sems = refs[:-2], refs[-2], refs[-1]
    copies = []
    for piece in pieces:
        for j in range(piece.shape[0]):
            n = len(copies)
            copies.append(pltpu.make_async_copy(piece.at[j], out.at[place[n]], sems.at[n]))
    for c in copies:
        c.start()
    for c in copies:
        c.wait()


def scatter_more_kernel(place, base, *refs):
    del base
    scatter_kernel(place, *refs)


def scatter_blocks(place, pieces, out_shape, base=None):
    count = sum(p.shape[0] for p in pieces)
    operands = list(pieces) if base is None else [base] + list(pieces)
    return pl.pallas_call(
        scatter_kernel if base is None else scatter_more_kernel,
        out_shape=out_shape,
        in_specs=[SMEM] + [ANY] * (len(operands) - len(pieces)) + [pl.BlockSpec(memory_space=pltpu.VMEM)] * len(pieces),
        out_specs=ANY,
        scratch_shapes=[pltpu.SemaphoreType.DMA((count,))],
        input_output_aliases={} if base is None else {1: 0},
    )(place, *operands)


def body(gradients, second_moment, inverse_roots, owners, weights):
    groups = lax.axis_size("groups")
    shards = lax.axis_size("shard")
    g = lax.axis_index("groups")
    total_blocks = owners.shape[0]
    nbg = total_blocks // groups
    slots = inverse_roots.shape[2]
    rows = gradients.shape[2]
    width = gradients.shape[3]
    half = nbg // 2

    def shift(n):
        return [(i, (i + n) % groups) for i in range(groups)]

    starts = [sum(CHUNKS[:c]) for c in range(len(CHUNKS))]
    received = []
    grads = gradients
    for start, per in zip(starts, CHUNKS):
        pieces = [
            lax.dynamic_slice(grads[0], (nbg * ((g + n) % groups), start, 0), (nbg, per, width)) for n in (1, 3, 2)
        ]
        grads, pieces = lax.optimization_barrier((grads, pieces))
        received.append([lax.ppermute(p, "groups", shift(n)) for p, n in zip(pieces, (1, 3, 2))])

    grouped = owners.reshape(groups, nbg)
    same = grouped[:, :, None] == grouped[:, None, :]
    ids = jnp.arange(nbg, dtype=jnp.int32)
    earlier = ids[None, :] < ids[:, None]
    rank = jnp.sum((same & earlier[None]).astype(jnp.int32), axis=2)
    firsts = rank == 0
    before = jnp.sum((firsts[:, None, :] & earlier[None]).astype(jnp.int32), axis=2)
    n_first = jnp.sum(firsts.astype(jnp.int32), axis=1, keepdims=True)
    spot = jnp.where(firsts, before, n_first + ids[None] - before)
    sits = spot[:, None, :] == ids[None, :, None]
    order = jnp.sum(jnp.where(sits, ids[None, None, :], 0), axis=2)
    by_order = [
        lax.dynamic_index_in_dim(jnp.sum(jnp.where(sits, t[:, None, :], 0), axis=2), g, 0, False)
        for t in (jnp.broadcast_to(ids[None], grouped.shape), grouped, rank)
    ]
    my_owner = lax.dynamic_index_in_dim(grouped, g, 0, False)
    my_rank = lax.dynamic_index_in_dim(rank, g, 0, False)
    dest = jnp.arange(shards, dtype=jnp.int32)
    match = [(my_owner[None, :] == dest[:, None]) & (my_rank[None, :] == k) for k in range(slots)]
    source = [jnp.sum(jnp.where(m, ids[None], 0), axis=1) for m in match]

    def exchange(x, after=None):
        if after is not None:
            x, after = lax.optimization_barrier((x, after))
        return lax.all_to_all(x, "shard", 0, 0, tiled=True)

    norm = None
    coded = []
    for c, start in enumerate(starts):
        last = c == len(starts) - 1
        wanted = source if last else [jnp.stack(source, 1).reshape(-1)]
        code = sum_replicas(gradients, received[c], second_moment, start, g, wanted, norm, last)
        coded.append(code)
        norm = None if last else code[-1]
    early = []
    for c, code in enumerate(coded[:-1]):
        packed = code[0].reshape(shards, slots, CHUNKS[c], width + LANES)
        early.append(exchange(packed, early[-1] if early else None))
    arrived = []
    for k in range(slots):
        arrived.append(early + [exchange(coded[-1][k], arrived[-1][-1] if k else early[-1])])

    backs = []
    for k in range(slots):
        update = owner_work(inverse_roots, arrived[k], k)
        backs.append(exchange(update.reshape(shards, rows, width), backs[-1] if k else None))

    def to_all(new):
        a, b = new
        prev_a = lax.ppermute(a, "groups", shift(1))
        after_b = lax.ppermute(b, "groups", shift(3))
        prev_b = lax.ppermute(b, "groups", shift(1))
        after_a = lax.ppermute(a, "groups", shift(3))
        far_a = lax.ppermute(prev_a, "groups", shift(1))
        far_b = lax.ppermute(after_b, "groups", shift(3))
        return [a, b, prev_a, prev_b, after_a, after_b, far_a, far_b]

    def places(lo, hi):
        out = []
        for n in (0, 3, 1, 2):
            h = (g + n) % groups
            out.append(nbg * h + lax.dynamic_index_in_dim(order, h, 0, False)[lo:hi])
        return jnp.concatenate(out)

    def table(lo, hi):
        return jnp.concatenate([t[lo:hi] for t in by_order])

    out_shape = jax.ShapeDtypeStruct((total_blocks, rows, width), jnp.bfloat16)
    new = renew(table(0, half), weights, backs[:1])
    pieces0 = to_all(new)
    late = pass_table(table(half, nbg), pieces0[2], pieces0[5])
    new = renew(late, weights, backs)
    pieces1 = to_all(new)
    out = scatter_blocks(places(0, half), pieces0, out_shape)
    where = places(half, nbg)
    far = 3 * half
    out = scatter_blocks(where[:far], pieces1[:6], out_shape, base=out)
    return scatter_blocks(where[far:], pieces1[6:], out_shape, base=out)


def solution(mesh):
    return jax.shard_map(
        body,
        mesh=mesh,
        in_specs=(
            P("groups", None, "shard", None),
            P("groups", "shard", None),
            P("groups", "shard", None, None, None, None),
            P(),
            P("groups", "shard", None),
        ),
        out_specs=P(None, "shard", None),
        check_vma=False,
    )
```

```python
import functools

import jax
import jax.numpy as jnp
from jax import lax
from jax.experimental import pallas as pl
from jax.experimental.pallas import tpu as pltpu
from jax.sharding import PartitionSpec as P


LANES = 128
CHUNKS = (8, 8, 16)
TALL = 256
ANY = pl.BlockSpec(memory_space=pl.ANY)
SMEM = pl.BlockSpec(memory_space=pltpu.SMEM)
SMALL = pltpu.CompilerParams(vmem_limit_bytes=12 * 2**20)
LARGE = pltpu.CompilerParams(vmem_limit_bytes=20 * 2**20)
VMEM = pl.BlockSpec(memory_space=pltpu.VMEM)


def in_hbm(x):
    return pltpu.with_memory_space_constraint(x, pltpu.HBM)


def in_vmem(x):
    return pltpu.with_memory_space_constraint(x, pltpu.VMEM)


def two_parts(values):
    high = values.astype(jnp.bfloat16)
    low = (values - high.astype(jnp.float32)).astype(jnp.bfloat16)
    return high, low


def dot(a, b):
    return jnp.dot(a, b, preferred_element_type=jnp.float32)


def sum_kernel(start, first, last, meta, gradients, one, two, three, old_all, *refs):
    before = None if first else refs[0]
    outs = refs[0 if first else 1 : -5]
    norms = None if last else outs[-1]
    outs = outs if last else outs[:-1]
    own, old, codes, in_sems, sems = refs[-5:]
    nbg, per, width = one.shape
    rows = pl.ds(start, per)
    loads = [
        pltpu.make_async_copy(gradients.at[0, pl.ds(meta[0] * nbg, nbg), rows], own, in_sems.at[0]),
        pltpu.make_async_copy(old_all.at[:, rows], old, in_sems.at[1]),
    ]
    for x in loads:
        x.start()
    for x in loads:
        x.wait()

    def code_block(at):
        total = (own[at].astype(jnp.float32) + one[at].astype(jnp.float32)) + (
            two[at].astype(jnp.float32) + three[at].astype(jnp.float32)
        )
        moment = 0.95 * old[at].astype(jnp.float32) + 0.05 * total * total
        adam = total / (moment * lax.rsqrt(moment) + 1e-08)
        adam = adam * adam
        parts = [total[:, j : j + LANES] for j in range(0, width, LANES)]
        top = functools.reduce(jnp.maximum, [jnp.abs(p) for p in parts])
        if last:
            top = jnp.maximum(top[:8], top[8:])
        power = jnp.floor(jnp.log2(jnp.maximum(top, 1e-30)) + 1e-4) - 14.0
        grow = jnp.exp2(-power)
        if last:
            grow = jnp.concatenate([grow, grow], axis=0)
        for j, p in enumerate(parts):
            codes[at, :, j * LANES : (j + 1) * LANES] = jnp.round(p * grow).astype(jnp.int32).astype(jnp.int16)
        squares = functools.reduce(jnp.add, [adam[:, j : j + LANES] for j in range(0, width, LANES)])
        squares = jnp.sum(squares, axis=0, keepdims=True)
        if not first:
            squares = squares + before[at]
        if not last:
            norms[at] = squares
            codes[at, :, width:] = power.astype(jnp.int32).astype(jnp.int16)
            return
        scale = jnp.ceil(jnp.log2(jnp.maximum(squares, 1e-30)))
        scaled = squares * jnp.exp2(14.0 - scale)
        high = jnp.floor(scaled)
        low = jnp.floor((scaled - high) * 16384.0)
        row = lax.broadcasted_iota(jnp.int32, (8, LANES), 0)
        full = jnp.where(row == 0, scale, jnp.where(row == 1, high, low))
        full = jnp.concatenate([power, full], axis=0)
        codes[at, :, width:] = full.astype(jnp.int32).astype(jnp.int16)

    def block(at, _):
        code_block(at)
        owner, rank = meta[1 + at], meta[1 + nbg + at]
        if not last:
            slots = outs[0].shape[1]
            pltpu.make_async_copy(codes.at[at], outs[0].at[owner, jnp.minimum(rank, slots - 1)], sems.at[at]).start()
        else:
            for k, out in enumerate(outs):

                @pl.when(rank == k)
                def _():
                    pltpu.make_async_copy(codes.at[at], out.at[owner], sems.at[at]).start()

        return 0

    lax.fori_loop(0, nbg, block, 0)
    to = outs[0].at[0] if last else outs[0].at[0, 0]
    for n in range(nbg):
        pltpu.make_async_copy(codes.at[n], to, sems.at[n]).wait()


def sum_replicas(gradients, received, old, start, meta, before, shards, slots, last):
    nbg, per, width = received[0].shape
    columns = width + LANES
    if last:
        shapes = [jax.ShapeDtypeStruct((shards, per, columns), jnp.int16)] * slots
    else:
        shapes = [
            jax.ShapeDtypeStruct((shards, slots, per, columns), jnp.int16),
            jax.ShapeDtypeStruct((nbg, 1, LANES), jnp.float32),
        ]
    carried = [] if before is None else [before]
    return pl.pallas_call(
        functools.partial(sum_kernel, start, before is None, last),
        out_shape=shapes,
        in_specs=[SMEM, ANY, VMEM, VMEM, VMEM, ANY] + [VMEM] * len(carried),
        out_specs=[ANY] * slots if last else [ANY, VMEM],
        scratch_shapes=[
            pltpu.VMEM((nbg, per, width), jnp.bfloat16),
            pltpu.VMEM((nbg, per, width), jnp.bfloat16),
            pltpu.VMEM((nbg, per, columns), jnp.int16),
            pltpu.SemaphoreType.DMA((2,)),
            pltpu.SemaphoreType.DMA((nbg,)),
        ],
        compiler_params=SMALL,
    )(meta, in_hbm(gradients), *[in_vmem(r) for r in received], in_hbm(old), *carried)


def owner_kernel(slot, all_roots, *refs):
    arrived, update, high, low, pre, roots, sems = refs[:-6], *refs[-6:]
    width = update.shape[0]
    loads = [pltpu.make_async_copy(all_roots.at[0, 0, slot, k], roots.at[k], sems.at[k]) for k in (1, 0)]
    for x in loads:
        x.start()
    n_src = arrived[0].shape[0]
    early, final = arrived[:-1], arrived[-1]
    top = sum(a.shape[-2] for a in early)
    rows = top + final.shape[-2]

    def step_of(powers):
        return jnp.exp2(powers.astype(jnp.int32).astype(jnp.float32))

    def unpack(n, graft):
        at = pl.ds(pl.multiple_of(n * rows, rows), top)
        got = [a[n, slot] for a in early]
        steps = [step_of(x[:, width:]) for x in got]
        for j in range(0, width, LANES):
            value = [x[:, j : j + LANES].astype(jnp.int32).astype(jnp.float32) * t for x, t in zip(got, steps)]
            high[at, j : j + LANES], low[at, j : j + LANES] = two_parts(jnp.concatenate(value, axis=0))
        at = pl.ds(pl.multiple_of(n * rows + top, top), rows - top)
        got = final[n]
        tail = got[:, width:].astype(jnp.int32).astype(jnp.float32)
        step = jnp.exp2(tail[:8])
        step = jnp.concatenate([step, step], axis=0)
        for j in range(0, width, LANES):
            value = got[:, j : j + LANES].astype(jnp.int32).astype(jnp.float32) * step
            high[at, j : j + LANES], low[at, j : j + LANES] = two_parts(value)
        return graft + jnp.exp2(tail[8:9] - 14.0) * (tail[9:10] + tail[10:11] * (1.0 / 16384.0))

    graft = lax.fori_loop(0, n_src, unpack, jnp.zeros((1, LANES), jnp.float32))
    graft = jnp.sum(graft, axis=1, keepdims=True)
    loads[0].wait()
    right = roots[1]
    for m in range(0, width, TALL):
        at = pl.ds(m, TALL)
        high[at, :], low[at, :] = two_parts(dot(high[at, :], right) + dot(low[at, :], right))
    loads[1].wait()
    square = jnp.zeros((1, width), jnp.float32)
    for m in range(0, width, TALL):
        at = pl.ds(m, TALL)
        left = roots[0, at, :]
        got = dot(left, high[...]) + dot(left, low[...])
        pre[at, :] = got
        square = square + jnp.sum(got * got, axis=0, keepdims=True)
    square = jnp.sum(square, axis=1, keepdims=True)
    scale = jnp.sqrt(graft) / jnp.sqrt(square + 1e-06)
    for m in range(0, width, TALL):
        at = pl.ds(m, TALL)
        update[at, :] = (scale * pre[at, :]).astype(jnp.bfloat16)


def owner_work(roots, arrived, slot):
    width = roots.shape[-1]
    return pl.pallas_call(
        functools.partial(owner_kernel, slot),
        out_shape=jax.ShapeDtypeStruct((width, width), jnp.bfloat16),
        in_specs=[ANY] + [VMEM] * len(arrived),
        out_specs=VMEM,
        scratch_shapes=[
            pltpu.VMEM((width, width), jnp.bfloat16),
            pltpu.VMEM((width, width), jnp.bfloat16),
            pltpu.VMEM((width, width), jnp.float32),
            pltpu.VMEM((2, width, width), jnp.bfloat16),
            pltpu.SemaphoreType.DMA((2,)),
        ],
        compiler_params=LARGE,
    )(in_hbm(roots), *[in_vmem(a) for a in arrived])


def renew_kernel(count, table, weights, *refs):
    backs, outs, held, sems = refs[:-4], refs[-4:-2], refs[-2], refs[-1]
    copies = [pltpu.make_async_copy(weights.at[table[j]], held.at[j], sems.at[j]) for j in range(count)]
    for c in copies:
        c.start()
    half = count // 2

    def block(j, k):
        grad = backs[k][table[count + j]].astype(jnp.float32)
        stepped = held[j].astype(jnp.float32) - 0.5 * grad
        scale = lax.rsqrt(jnp.mean(stepped * stepped, axis=1, keepdims=True) + 1e-06)
        outs[j // half][j % half] = (stepped * scale).astype(jnp.bfloat16)

    for j in range(count):
        copies[j].wait()
        if len(backs) == 1:
            block(j, 0)
            continue
        for k in range(len(backs)):
            pl.when(table[2 * count + j] == k)(functools.partial(block, j, k))


def renew(table, weights, backs):
    count = table.shape[0] // 3
    rows, width = weights.shape[1:]
    half = jax.ShapeDtypeStruct((count // 2, rows, width), jnp.bfloat16)
    return pl.pallas_call(
        functools.partial(renew_kernel, count),
        out_shape=(half, half),
        in_specs=[SMEM, ANY] + [VMEM] * len(backs),
        scratch_shapes=[
            pltpu.VMEM((count, rows, width), jnp.bfloat16),
            pltpu.SemaphoreType.DMA((count,)),
        ],
        compiler_params=SMALL,
    )(table, in_hbm(weights), *[in_vmem(x) for x in backs])


def pass_kernel(count, *refs):
    for ref, out in zip(refs[:count], refs[-count:]):
        for j in range(ref.shape[0]):
            out[j] = ref[j]


def pass_tables(tables, after=()):
    return pl.pallas_call(
        functools.partial(pass_kernel, len(tables)),
        out_shape=[jax.ShapeDtypeStruct(t.shape, t.dtype) for t in tables],
        in_specs=[SMEM] * len(tables) + [VMEM] * len(after),
        out_specs=[SMEM] * len(tables),
        compiler_params=SMALL,
    )(*tables, *[in_vmem(a) for a in after])


def scatter_kernel(place, *refs):
    pieces, out, sems = refs[:-2], refs[-2], refs[-1]
    copies = []
    for piece in pieces:
        for j in range(piece.shape[0]):
            n = len(copies)
            copies.append(pltpu.make_async_copy(piece.at[j], out.at[place[n]], sems.at[n]))
    for c in copies:
        c.start()
    for c in copies:
        c.wait()


def scatter_more_kernel(place, base, *refs):
    del base
    scatter_kernel(place, *refs)


def scatter_blocks(place, pieces, out_shape, base=None):
    pieces = [in_vmem(p) for p in pieces]
    count = sum(p.shape[0] for p in pieces)
    operands = pieces if base is None else [in_hbm(base)] + pieces
    return pl.pallas_call(
        scatter_kernel if base is None else scatter_more_kernel,
        out_shape=out_shape,
        in_specs=[SMEM] + [ANY] * (len(operands) - len(pieces)) + [pl.BlockSpec(memory_space=pltpu.VMEM)] * len(pieces),
        out_specs=ANY,
        scratch_shapes=[pltpu.SemaphoreType.DMA((count,))],
        input_output_aliases={} if base is None else {1: 0},
        compiler_params=SMALL,
    )(place, *operands)


def body(gradients, second_moment, inverse_roots, owners, weights):
    groups = lax.axis_size("groups")
    shards = lax.axis_size("shard")
    g = lax.axis_index("groups")
    total_blocks = owners.shape[0]
    nbg = total_blocks // groups
    slots = inverse_roots.shape[2]
    rows = gradients.shape[2]
    width = gradients.shape[3]
    half = nbg // 2

    def shift(n):
        return [(i, (i + n) % groups) for i in range(groups)]

    starts = [sum(CHUNKS[:c]) for c in range(len(CHUNKS))]
    received = []
    grads = gradients
    for start, per in zip(starts, CHUNKS):
        pieces = [
            lax.dynamic_slice(grads[0], (nbg * ((g + n) % groups), start, 0), (nbg, per, width)) for n in (1, 3, 2)
        ]
        grads, pieces = lax.optimization_barrier((grads, pieces))
        received.append([lax.ppermute(p, "groups", shift(n)) for p, n in zip(pieces, (1, 3, 2))])

    ids = jnp.arange(nbg, dtype=jnp.int32)
    earlier = ids[None, :] < ids[:, None]
    my_owner = lax.dynamic_slice_in_dim(owners, nbg * g, nbg)
    my_rank = jnp.sum(((my_owner[:, None] == my_owner[None, :]) & earlier).astype(jnp.int32), axis=1)
    meta = jnp.concatenate([g[None].astype(jnp.int32), my_owner, my_rank])
    grouped = owners.reshape(groups, nbg)
    same = grouped[:, :, None] == grouped[:, None, :]
    rank = jnp.sum((same & earlier[None]).astype(jnp.int32), axis=2)
    firsts = rank == 0
    before = jnp.sum((firsts[:, None, :] & earlier[None]).astype(jnp.int32), axis=2)
    n_first = jnp.sum(firsts.astype(jnp.int32), axis=1, keepdims=True)
    spot = jnp.where(firsts, before, n_first + ids[None] - before)
    sits = spot[:, None, :] == ids[None, :, None]
    order = jnp.sum(jnp.where(sits, ids[None, None, :], 0), axis=2)
    by_order = [
        lax.dynamic_index_in_dim(jnp.sum(jnp.where(sits, t[:, None, :], 0), axis=2), g, 0, False)
        for t in (jnp.broadcast_to(ids[None], grouped.shape), grouped, rank)
    ]

    def exchange(x, after=None):
        if after is not None:
            x, after = lax.optimization_barrier((x, after))
        return lax.all_to_all(x, "shard", 0, 0, tiled=True)

    norm = None
    coded = []
    for c, start in enumerate(starts):
        last = c == len(starts) - 1
        code = sum_replicas(gradients, received[c], second_moment, start, meta, norm, shards, slots, last)
        coded.append(code)
        norm = None if last else code[-1]
    early = []
    for code in coded[:-1]:
        early.append(exchange(code[0], early[-1] if early else None))
    arrived = []
    for k in range(slots):
        arrived.append(early + [exchange(coded[-1][k], arrived[-1][-1] if k else early[-1])])

    backs = []
    for k in range(slots):
        update = owner_work(inverse_roots, arrived[k], k)
        backs.append(exchange(update.reshape(shards, rows, width), backs[-1] if k else None))

    def to_all(new):
        a, b = new
        prev_a = lax.ppermute(a, "groups", shift(1))
        after_b = lax.ppermute(b, "groups", shift(3))
        prev_b = lax.ppermute(b, "groups", shift(1))
        after_a = lax.ppermute(a, "groups", shift(3))
        far_a = lax.ppermute(prev_a, "groups", shift(1))
        far_b = lax.ppermute(after_b, "groups", shift(3))
        return [a, b, prev_a, prev_b, after_a, after_b, far_a, far_b]

    def places(lo, hi):
        out = []
        for n in (0, 3, 1, 2):
            h = (g + n) % groups
            out.append(nbg * h + lax.dynamic_index_in_dim(order, h, 0, False)[lo:hi])
        return jnp.concatenate(out)

    def table(lo, hi):
        return jnp.concatenate([t[lo:hi] for t in by_order])

    out_shape = jax.ShapeDtypeStruct((total_blocks, rows, width), jnp.bfloat16)
    where = places(half, nbg)
    far = 3 * half
    tables = [table(0, half), table(half, nbg), places(0, half), where[:far], where[far:]]
    tables = pass_tables(tables)
    new = renew(tables[0], weights, backs[:1])
    pieces0 = to_all(new)
    late = pass_tables(tables[1:2], [pieces0[2], pieces0[5]])
    new = renew(late[0], weights, backs)
    pieces1 = to_all(new)
    out = scatter_blocks(tables[2], pieces0, out_shape)
    out = scatter_blocks(tables[3], pieces1[:6], out_shape, base=out)
    return scatter_blocks(tables[4], pieces1[6:], out_shape, base=out)


def solution(mesh):
    return jax.shard_map(
        body,
        mesh=mesh,
        in_specs=(
            P("groups", None, "shard", None),
            P("groups", "shard", None),
            P("groups", "shard", None, None, None, None),
            P(),
            P("groups", "shard", None),
        ),
        out_specs=P(None, "shard", None),
        check_vma=False,
    )
```

```python
import functools

import jax
import jax.numpy as jnp
from jax import lax
from jax.experimental import pallas as pl
from jax.experimental.pallas import tpu as pltpu
from jax.sharding import PartitionSpec as P


LANES = 128
CHUNKS = (8, 8, 8, 8)
TALL = 256
ANY = pl.BlockSpec(memory_space=pl.ANY)
SMEM = pl.BlockSpec(memory_space=pltpu.SMEM)
SMALL = pltpu.CompilerParams(vmem_limit_bytes=12 * 2**20)
LARGE = pltpu.CompilerParams(vmem_limit_bytes=20 * 2**20)
VMEM = pl.BlockSpec(memory_space=pltpu.VMEM)


def in_hbm(x):
    return pltpu.with_memory_space_constraint(x, pltpu.HBM)


def in_vmem(x):
    return pltpu.with_memory_space_constraint(x, pltpu.VMEM)


def two_parts(values):
    high = values.astype(jnp.bfloat16)
    low = (values - high.astype(jnp.float32)).astype(jnp.bfloat16)
    return high, low


def dot(a, b):
    return jnp.dot(a, b, preferred_element_type=jnp.float32)


def sum_kernel(start, first, last, meta, gradients, one, two, three, old_all, *refs):
    before = None if first else refs[0]
    outs = refs[0 if first else 1 : -5]
    norms = None if last else outs[-1]
    outs = outs if last else outs[:-1]
    own, old, codes, in_sems, sems = refs[-5:]
    nbg, per, width = one.shape
    rows = pl.ds(start, per)
    loads = [
        pltpu.make_async_copy(gradients.at[0, pl.ds(meta[0] * nbg, nbg), rows], own, in_sems.at[0]),
        pltpu.make_async_copy(old_all.at[:, rows], old, in_sems.at[1]),
    ]
    for x in loads:
        x.start()
    for x in loads:
        x.wait()

    def code_block(at):
        total = (own[at].astype(jnp.float32) + one[at].astype(jnp.float32)) + (
            two[at].astype(jnp.float32) + three[at].astype(jnp.float32)
        )
        moment = 0.95 * old[at].astype(jnp.float32) + 0.05 * total * total
        adam = total / (moment * lax.rsqrt(moment) + 1e-08)
        adam = adam * adam
        parts = [total[:, j : j + LANES] for j in range(0, width, LANES)]
        top = functools.reduce(jnp.maximum, [jnp.abs(p) for p in parts])
        if last:
            top = jnp.maximum(top, pltpu.roll(top, 4, 0))
        power = jnp.floor(jnp.log2(jnp.maximum(top, 1e-30)) + 1e-4) - 14.0
        grow = jnp.exp2(-power)
        for j, p in enumerate(parts):
            codes[at, :, j * LANES : (j + 1) * LANES] = jnp.round(p * grow).astype(jnp.int32).astype(jnp.int16)
        squares = functools.reduce(jnp.add, [adam[:, j : j + LANES] for j in range(0, width, LANES)])
        squares = jnp.sum(squares, axis=0, keepdims=True)
        if not first:
            squares = squares + before[at]
        if not last:
            norms[at] = squares
            codes[at, :, width:] = power.astype(jnp.int32).astype(jnp.int16)
            return
        scale = jnp.ceil(jnp.log2(jnp.maximum(squares, 1e-30)))
        scaled = squares * jnp.exp2(14.0 - scale)
        high = jnp.floor(scaled)
        low = jnp.floor((scaled - high) * 16384.0)
        row = lax.broadcasted_iota(jnp.int32, power.shape, 0)
        full = jnp.where(row < 4, power, jnp.where(row == 4, scale, jnp.where(row == 5, high, low)))
        codes[at, :, width:] = full.astype(jnp.int32).astype(jnp.int16)

    def block(at, _):
        code_block(at)
        owner, rank = meta[1 + at], meta[1 + nbg + at]
        if not last:
            slots = outs[0].shape[1]
            pltpu.make_async_copy(codes.at[at], outs[0].at[owner, jnp.minimum(rank, slots - 1)], sems.at[at]).start()
        else:
            for k, out in enumerate(outs):

                @pl.when(rank == k)
                def _():
                    pltpu.make_async_copy(codes.at[at], out.at[owner], sems.at[at]).start()

        return 0

    lax.fori_loop(0, nbg, block, 0)
    to = outs[0].at[0] if last else outs[0].at[0, 0]
    for n in range(nbg):
        pltpu.make_async_copy(codes.at[n], to, sems.at[n]).wait()


def sum_replicas(gradients, received, old, start, meta, before, shards, slots, last):
    nbg, per, width = received[0].shape
    columns = width + LANES
    if last:
        shapes = [jax.ShapeDtypeStruct((shards, per, columns), jnp.int16)] * slots
    else:
        shapes = [
            jax.ShapeDtypeStruct((shards, slots, per, columns), jnp.int16),
            jax.ShapeDtypeStruct((nbg, 1, LANES), jnp.float32),
        ]
    carried = [] if before is None else [before]
    return pl.pallas_call(
        functools.partial(sum_kernel, start, before is None, last),
        out_shape=shapes,
        in_specs=[SMEM, ANY, VMEM, VMEM, VMEM, ANY] + [VMEM] * len(carried),
        out_specs=[ANY] * slots if last else [ANY, VMEM],
        scratch_shapes=[
            pltpu.VMEM((nbg, per, width), jnp.bfloat16),
            pltpu.VMEM((nbg, per, width), jnp.bfloat16),
            pltpu.VMEM((nbg, per, columns), jnp.int16),
            pltpu.SemaphoreType.DMA((2,)),
            pltpu.SemaphoreType.DMA((nbg,)),
        ],
        compiler_params=SMALL,
    )(meta, in_hbm(gradients), *[in_vmem(r) for r in received], in_hbm(old), *carried)


def owner_kernel(slot, all_roots, *refs):
    arrived, update, high, low, pre, roots, sems = refs[:-6], *refs[-6:]
    width = update.shape[0]
    loads = [pltpu.make_async_copy(all_roots.at[0, 0, slot, k], roots.at[k], sems.at[k]) for k in (1, 0)]
    for x in loads:
        x.start()
    n_src = arrived[0].shape[0]
    per = arrived[0].shape[-2]
    rows = per * len(arrived)

    def unpack(n, graft):
        codes = [a[n, slot] if len(a.shape) == 4 else a[n] for a in arrived]
        tails = [x[:, width:].astype(jnp.int32).astype(jnp.float32) for x in codes]
        norm = tails[-1]
        row = lax.broadcasted_iota(jnp.int32, norm.shape, 0)
        tails[-1] = jnp.where(row < 4, norm, pltpu.roll(norm, 4, 0))
        steps = [jnp.exp2(t) for t in tails]
        for c in range(0, len(codes), 2):
            at = pl.ds(pl.multiple_of(n * rows + c * per, 2 * per), 2 * per)
            for j in range(0, width, LANES):
                value = [x[:, j : j + LANES].astype(jnp.int32).astype(jnp.float32) * t for x, t in zip(codes[c : c + 2], steps[c : c + 2])]
                high[at, j : j + LANES], low[at, j : j + LANES] = two_parts(jnp.concatenate(value, axis=0))
        return graft + jnp.exp2(norm[4:5] - 14.0) * (norm[5:6] + norm[6:7] * (1.0 / 16384.0))

    graft = lax.fori_loop(0, n_src, unpack, jnp.zeros((1, LANES), jnp.float32))
    graft = jnp.sum(graft, axis=1, keepdims=True)
    loads[0].wait()
    right = roots[1]
    for m in range(0, width, TALL):
        at = pl.ds(m, TALL)
        high[at, :], low[at, :] = two_parts(dot(high[at, :], right) + dot(low[at, :], right))
    loads[1].wait()
    square = jnp.zeros((1, width), jnp.float32)
    for m in range(0, width, TALL):
        at = pl.ds(m, TALL)
        left = roots[0, at, :]
        got = dot(left, high[...]) + dot(left, low[...])
        pre[at, :] = got
        square = square + jnp.sum(got * got, axis=0, keepdims=True)
    square = jnp.sum(square, axis=1, keepdims=True)
    scale = jnp.sqrt(graft) / jnp.sqrt(square + 1e-06)
    for m in range(0, width, TALL):
        at = pl.ds(m, TALL)
        update[at, :] = (scale * pre[at, :]).astype(jnp.bfloat16)


def owner_work(roots, arrived, slot):
    width = roots.shape[-1]
    return pl.pallas_call(
        functools.partial(owner_kernel, slot),
        out_shape=jax.ShapeDtypeStruct((width, width), jnp.bfloat16),
        in_specs=[ANY] + [VMEM] * len(arrived),
        out_specs=VMEM,
        scratch_shapes=[
            pltpu.VMEM((width, width), jnp.bfloat16),
            pltpu.VMEM((width, width), jnp.bfloat16),
            pltpu.VMEM((width, width), jnp.float32),
            pltpu.VMEM((2, width, width), jnp.bfloat16),
            pltpu.SemaphoreType.DMA((2,)),
        ],
        compiler_params=LARGE,
    )(in_hbm(roots), *[in_vmem(a) for a in arrived])


def renew_kernel(count, table, weights, *refs):
    backs, outs, held, sems = refs[:-4], refs[-4:-2], refs[-2], refs[-1]
    copies = [pltpu.make_async_copy(weights.at[table[j]], held.at[j], sems.at[j]) for j in range(count)]
    for c in copies:
        c.start()
    half = count // 2

    def block(j, k):
        grad = backs[k][table[count + j]].astype(jnp.float32)
        stepped = held[j].astype(jnp.float32) - 0.5 * grad
        scale = lax.rsqrt(jnp.mean(stepped * stepped, axis=1, keepdims=True) + 1e-06)
        outs[j // half][j % half] = (stepped * scale).astype(jnp.bfloat16)

    for j in range(count):
        copies[j].wait()
        if len(backs) == 1:
            block(j, 0)
            continue
        for k in range(len(backs)):
            pl.when(table[2 * count + j] == k)(functools.partial(block, j, k))


def renew(table, weights, backs):
    count = table.shape[0] // 3
    rows, width = weights.shape[1:]
    half = jax.ShapeDtypeStruct((count // 2, rows, width), jnp.bfloat16)
    return pl.pallas_call(
        functools.partial(renew_kernel, count),
        out_shape=(half, half),
        in_specs=[SMEM, ANY] + [VMEM] * len(backs),
        scratch_shapes=[
            pltpu.VMEM((count, rows, width), jnp.bfloat16),
            pltpu.SemaphoreType.DMA((count,)),
        ],
        compiler_params=SMALL,
    )(table, in_hbm(weights), *[in_vmem(x) for x in backs])


def pass_kernel(count, *refs):
    for ref, out in zip(refs[:count], refs[-count:]):
        for j in range(ref.shape[0]):
            out[j] = ref[j]


def pass_tables(tables, after=()):
    return pl.pallas_call(
        functools.partial(pass_kernel, len(tables)),
        out_shape=[jax.ShapeDtypeStruct(t.shape, t.dtype) for t in tables],
        in_specs=[SMEM] * len(tables) + [VMEM] * len(after),
        out_specs=[SMEM] * len(tables),
        compiler_params=SMALL,
    )(*tables, *[in_vmem(a) for a in after])


def scatter_kernel(place, *refs):
    pieces, out, sems = refs[:-2], refs[-2], refs[-1]
    copies = []
    for piece in pieces:
        for j in range(piece.shape[0]):
            n = len(copies)
            copies.append(pltpu.make_async_copy(piece.at[j], out.at[place[n]], sems.at[n]))
    for c in copies:
        c.start()
    for c in copies:
        c.wait()


def scatter_more_kernel(place, base, *refs):
    del base
    scatter_kernel(place, *refs)


def scatter_blocks(place, pieces, out_shape, base=None):
    pieces = [in_vmem(p) for p in pieces]
    count = sum(p.shape[0] for p in pieces)
    operands = pieces if base is None else [in_hbm(base)] + pieces
    return pl.pallas_call(
        scatter_kernel if base is None else scatter_more_kernel,
        out_shape=out_shape,
        in_specs=[SMEM] + [ANY] * (len(operands) - len(pieces)) + [pl.BlockSpec(memory_space=pltpu.VMEM)] * len(pieces),
        out_specs=ANY,
        scratch_shapes=[pltpu.SemaphoreType.DMA((count,))],
        input_output_aliases={} if base is None else {1: 0},
        compiler_params=SMALL,
    )(place, *operands)


def body(gradients, second_moment, inverse_roots, owners, weights):
    groups = lax.axis_size("groups")
    shards = lax.axis_size("shard")
    g = lax.axis_index("groups")
    total_blocks = owners.shape[0]
    nbg = total_blocks // groups
    slots = inverse_roots.shape[2]
    rows = gradients.shape[2]
    width = gradients.shape[3]
    half = nbg // 2

    def shift(n):
        return [(i, (i + n) % groups) for i in range(groups)]

    starts = [sum(CHUNKS[:c]) for c in range(len(CHUNKS))]
    received = []
    grads = gradients
    for start, per in zip(starts, CHUNKS):
        pieces = [
            lax.dynamic_slice(grads[0], (nbg * ((g + n) % groups), start, 0), (nbg, per, width)) for n in (1, 3, 2)
        ]
        grads, pieces = lax.optimization_barrier((grads, pieces))
        received.append([lax.ppermute(p, "groups", shift(n)) for p, n in zip(pieces, (1, 3, 2))])

    ids = jnp.arange(nbg, dtype=jnp.int32)
    earlier = ids[None, :] < ids[:, None]
    my_owner = lax.dynamic_slice_in_dim(owners, nbg * g, nbg)
    my_rank = jnp.sum(((my_owner[:, None] == my_owner[None, :]) & earlier).astype(jnp.int32), axis=1)
    meta = jnp.concatenate([g[None].astype(jnp.int32), my_owner, my_rank])
    grouped = owners.reshape(groups, nbg)
    same = grouped[:, :, None] == grouped[:, None, :]
    rank = jnp.sum((same & earlier[None]).astype(jnp.int32), axis=2)
    firsts = rank == 0
    before = jnp.sum((firsts[:, None, :] & earlier[None]).astype(jnp.int32), axis=2)
    n_first = jnp.sum(firsts.astype(jnp.int32), axis=1, keepdims=True)
    spot = jnp.where(firsts, before, n_first + ids[None] - before)
    sits = spot[:, None, :] == ids[None, :, None]
    order = jnp.sum(jnp.where(sits, ids[None, None, :], 0), axis=2)
    by_order = [
        lax.dynamic_index_in_dim(jnp.sum(jnp.where(sits, t[:, None, :], 0), axis=2), g, 0, False)
        for t in (jnp.broadcast_to(ids[None], grouped.shape), grouped, rank)
    ]

    def exchange(x, after=None):
        if after is not None:
            x, after = lax.optimization_barrier((x, after))
        return lax.all_to_all(x, "shard", 0, 0, tiled=True)

    norm = None
    coded = []
    for c, start in enumerate(starts):
        last = c == len(starts) - 1
        code = sum_replicas(gradients, received[c], second_moment, start, meta, norm, shards, slots, last)
        coded.append(code)
        norm = None if last else code[-1]
    early = []
    for code in coded[:-1]:
        early.append(exchange(code[0], early[-1] if early else None))
    arrived = []
    for k in range(slots):
        arrived.append(early + [exchange(coded[-1][k], arrived[-1][-1] if k else early[-1])])

    backs = []
    for k in range(slots):
        update = owner_work(inverse_roots, arrived[k], k)
        backs.append(exchange(update.reshape(shards, rows, width), backs[-1] if k else None))

    def to_all(new):
        a, b = new
        prev_a = lax.ppermute(a, "groups", shift(1))
        after_b = lax.ppermute(b, "groups", shift(3))
        prev_b = lax.ppermute(b, "groups", shift(1))
        after_a = lax.ppermute(a, "groups", shift(3))
        far_a = lax.ppermute(prev_a, "groups", shift(1))
        far_b = lax.ppermute(after_b, "groups", shift(3))
        return [a, b, prev_a, prev_b, after_a, after_b, far_a, far_b]

    def places(lo, hi):
        out = []
        for n in (0, 3, 1, 2):
            h = (g + n) % groups
            out.append(nbg * h + lax.dynamic_index_in_dim(order, h, 0, False)[lo:hi])
        return jnp.concatenate(out)

    def table(lo, hi):
        return jnp.concatenate([t[lo:hi] for t in by_order])

    out_shape = jax.ShapeDtypeStruct((total_blocks, rows, width), jnp.bfloat16)
    where = places(half, nbg)
    far = 3 * half
    tables = [table(0, half), table(half, nbg), places(0, half), where[:far], where[far:]]
    tables = pass_tables(tables)
    new = renew(tables[0], weights, backs[:1])
    pieces0 = to_all(new)
    late = pass_tables(tables[1:2], [pieces0[2], pieces0[5]])
    new = renew(late[0], weights, backs)
    pieces1 = to_all(new)
    out = scatter_blocks(tables[2], pieces0, out_shape)
    out = scatter_blocks(tables[3], pieces1[:6], out_shape, base=out)
    return scatter_blocks(tables[4], pieces1[6:], out_shape, base=out)


def solution(mesh):
    return jax.shard_map(
        body,
        mesh=mesh,
        in_specs=(
            P("groups", None, "shard", None),
            P("groups", "shard", None),
            P("groups", "shard", None, None, None, None),
            P(),
            P("groups", "shard", None),
        ),
        out_specs=P(None, "shard", None),
        check_vma=False,
    )
```

```python
import functools

import jax
import jax.numpy as jnp
from jax import lax
from jax.experimental import pallas as pl
from jax.experimental.pallas import tpu as pltpu
from jax.sharding import PartitionSpec as P


LANES = 128
CHUNKS = (8, 8, 8, 8)
TALL = 256
ANY = pl.BlockSpec(memory_space=pl.ANY)
SMEM = pl.BlockSpec(memory_space=pltpu.SMEM)
SMALL = pltpu.CompilerParams(vmem_limit_bytes=12 * 2**20)
LARGE = pltpu.CompilerParams(vmem_limit_bytes=20 * 2**20)
VMEM = pl.BlockSpec(memory_space=pltpu.VMEM)


def in_hbm(x):
    return pltpu.with_memory_space_constraint(x, pltpu.HBM)


def in_vmem(x):
    return pltpu.with_memory_space_constraint(x, pltpu.VMEM)


def two_parts(values):
    high = values.astype(jnp.bfloat16)
    low = (values - high.astype(jnp.float32)).astype(jnp.bfloat16)
    return high, low


def dot(a, b):
    return jnp.dot(a, b, preferred_element_type=jnp.float32)


def sum_kernel(start, offset, first, last, n_base, meta, gradients, one, two, three, old_all, *refs):
    before = None if first else refs[0]
    outs = refs[(0 if first else 1) + n_base : -5]
    norms = None if last else outs[-1]
    outs = outs if last else outs[:-1]
    own, old, codes, in_sems, sems = refs[-5:]
    nbg, per, width = one.shape
    rows = pl.ds(start, per)
    loads = [
        pltpu.make_async_copy(gradients.at[0, pl.ds(meta[0] * nbg, nbg), rows], own, in_sems.at[0]),
        pltpu.make_async_copy(old_all.at[:, rows], old, in_sems.at[1]),
    ]
    for x in loads:
        x.start()
    for x in loads:
        x.wait()

    def code_block(at):
        total = (own[at].astype(jnp.float32) + one[at].astype(jnp.float32)) + (
            two[at].astype(jnp.float32) + three[at].astype(jnp.float32)
        )
        moment = 0.95 * old[at].astype(jnp.float32) + 0.05 * total * total
        adam = total / (moment * lax.rsqrt(moment) + 1e-08)
        adam = adam * adam
        parts = [total[:, j : j + LANES] for j in range(0, width, LANES)]
        top = functools.reduce(jnp.maximum, [jnp.abs(p) for p in parts])
        if last:
            top = jnp.maximum(top, pltpu.roll(top, 4, 0))
        power = jnp.floor(jnp.log2(jnp.maximum(top, 1e-30)) + 1e-4) - 14.0
        grow = jnp.exp2(-power)
        for j, p in enumerate(parts):
            codes[at, :, j * LANES : (j + 1) * LANES] = jnp.round(p * grow).astype(jnp.int32).astype(jnp.int16)
        squares = functools.reduce(jnp.add, [adam[:, j : j + LANES] for j in range(0, width, LANES)])
        squares = jnp.sum(squares, axis=0, keepdims=True)
        if not first:
            squares = squares + before[at]
        if not last:
            norms[at] = squares
            codes[at, :, width:] = power.astype(jnp.int32).astype(jnp.int16)
            return
        scale = jnp.ceil(jnp.log2(jnp.maximum(squares, 1e-30)))
        scaled = squares * jnp.exp2(14.0 - scale)
        high = jnp.floor(scaled)
        low = jnp.floor((scaled - high) * 16384.0)
        row = lax.broadcasted_iota(jnp.int32, power.shape, 0)
        full = jnp.where(row < 4, power, jnp.where(row == 4, scale, jnp.where(row == 5, high, low)))
        codes[at, :, width:] = full.astype(jnp.int32).astype(jnp.int16)

    def block(at, _):
        code_block(at)
        owner, rank = meta[1 + at], meta[1 + nbg + at]
        if len(outs) == 1:
            to = outs[0].at[owner, jnp.minimum(rank, outs[0].shape[1] - 1), to_rows]
            pltpu.make_async_copy(codes.at[at], to, sems.at[at]).start()
        else:
            for k, out in enumerate(outs):

                @pl.when(rank == k)
                def _():
                    pltpu.make_async_copy(codes.at[at], out.at[owner, to_rows], sems.at[at]).start()

        return 0

    to_rows = pl.ds(offset, per)
    lax.fori_loop(0, nbg, block, 0)
    done = outs[0].at[0, 0, to_rows] if len(outs) == 1 else outs[0].at[0, to_rows]
    for n in range(nbg):
        pltpu.make_async_copy(codes.at[n], done, sems.at[n]).wait()


def sum_replicas(gradients, received, old, start, meta, before, last, offset, shapes, base):
    nbg, per, width = received[0].shape
    columns = width + LANES
    out_shapes = [pltpu.HBM(x, jnp.int16) for x in shapes]
    if not last:
        out_shapes.append(jax.ShapeDtypeStruct((nbg, 1, LANES), jnp.float32))
    carried = [] if before is None else [before]
    base = [in_hbm(x) for x in base]
    return pl.pallas_call(
        functools.partial(sum_kernel, start, offset, before is None, last, len(base)),
        out_shape=out_shapes,
        in_specs=[SMEM, ANY, VMEM, VMEM, VMEM, ANY] + [VMEM] * len(carried) + [ANY] * len(base),
        out_specs=[ANY] * len(shapes) + ([] if last else [VMEM]),
        scratch_shapes=[
            pltpu.VMEM((nbg, per, width), jnp.bfloat16),
            pltpu.VMEM((nbg, per, width), jnp.bfloat16),
            pltpu.VMEM((nbg, per, columns), jnp.int16),
            pltpu.SemaphoreType.DMA((2,)),
            pltpu.SemaphoreType.DMA((nbg,)),
        ],
        input_output_aliases={6 + len(carried) + n: n for n in range(len(base))},
        compiler_params=SMALL,
    )(meta, in_hbm(gradients), *[in_vmem(r) for r in received], in_hbm(old), *carried, *base)


def owner_kernel(slot, all_roots, *refs):
    early, late, out, high, low, pre, roots, update, sems, out_sems = refs
    width = update.shape[0]
    loads = [pltpu.make_async_copy(all_roots.at[0, 0, slot, k], roots.at[k], sems.at[k]) for k in (1, 0)]
    for x in loads:
        x.start()
    n_src, per = late.shape[:2]
    rows = 2 * per

    def unpack(n, graft):
        codes = [early[n, slot], late[n]]
        tails = [x[:, width:].astype(jnp.int32).astype(jnp.float32) for x in codes]
        norm = tails[1][8:]
        row = lax.broadcasted_iota(jnp.int32, norm.shape, 0)
        tails[1] = jnp.concatenate([tails[1][:8], jnp.where(row < 4, norm, pltpu.roll(norm, 4, 0))], axis=0)
        for c, (code, tail) in enumerate(zip(codes, tails)):
            at = pl.ds(pl.multiple_of(n * rows + c * per, per), per)
            step = jnp.exp2(tail)
            for j in range(0, width, LANES):
                value = code[:, j : j + LANES].astype(jnp.int32).astype(jnp.float32) * step
                high[at, j : j + LANES], low[at, j : j + LANES] = two_parts(value)
        return graft + jnp.exp2(norm[4:5] - 14.0) * (norm[5:6] + norm[6:7] * (1.0 / 16384.0))

    graft = lax.fori_loop(0, n_src, unpack, jnp.zeros((1, LANES), jnp.float32))
    graft = jnp.sum(graft, axis=1, keepdims=True)
    loads[0].wait()
    right = roots[1]
    for m in range(0, width, TALL):
        at = pl.ds(m, TALL)
        high[at, :], low[at, :] = two_parts(dot(high[at, :], right) + dot(low[at, :], right))
    loads[1].wait()
    square = jnp.zeros((1, width), jnp.float32)
    for m in range(0, width, TALL):
        at = pl.ds(m, TALL)
        left = roots[0, at, :]
        got = dot(left, high[...]) + dot(left, low[...])
        pre[at, :] = got
        square = square + jnp.sum(got * got, axis=0, keepdims=True)
    square = jnp.sum(square, axis=1, keepdims=True)
    scale = jnp.sqrt(graft) / jnp.sqrt(square + 1e-06)
    copies = []
    for n, m in enumerate(range(0, width, TALL)):
        at = pl.ds(m, TALL)
        update[at, :] = (scale * pre[at, :]).astype(jnp.bfloat16)
        copies.append(pltpu.make_async_copy(update.at[at], out.at[at], out_sems.at[n]))
        copies[-1].start()
    for c in copies:
        c.wait()


def owner_work(roots, arrived, slot):
    width = roots.shape[-1]
    return pl.pallas_call(
        functools.partial(owner_kernel, slot),
        out_shape=pltpu.HBM((width, width), jnp.bfloat16),
        in_specs=[ANY] + [VMEM] * len(arrived),
        out_specs=ANY,
        scratch_shapes=[
            pltpu.VMEM((width, width), jnp.bfloat16),
            pltpu.VMEM((width, width), jnp.bfloat16),
            pltpu.VMEM((width, width), jnp.float32),
            pltpu.VMEM((2, width, width), jnp.bfloat16),
            pltpu.VMEM((width, width), jnp.bfloat16),
            pltpu.SemaphoreType.DMA((2,)),
            pltpu.SemaphoreType.DMA((width // TALL,)),
        ],
        compiler_params=LARGE,
    )(in_hbm(roots), *[in_vmem(a) for a in arrived])


def renew_kernel(count, table, weights, *refs):
    backs, outs, held, sems = refs[:-4], refs[-4:-2], refs[-2], refs[-1]
    copies = [pltpu.make_async_copy(weights.at[table[j]], held.at[j], sems.at[j]) for j in range(count)]
    for c in copies:
        c.start()
    half = count // 2

    def block(j, k):
        grad = backs[k][table[count + j]].astype(jnp.float32)
        stepped = held[j].astype(jnp.float32) - 0.5 * grad
        scale = lax.rsqrt(jnp.mean(stepped * stepped, axis=1, keepdims=True) + 1e-06)
        outs[j // half][j % half] = (stepped * scale).astype(jnp.bfloat16)

    for j in range(count):
        copies[j].wait()
        if len(backs) == 1:
            block(j, 0)
            continue
        for k in range(len(backs)):
            pl.when(table[2 * count + j] == k)(functools.partial(block, j, k))


def renew(table, weights, backs):
    count = table.shape[0] // 3
    rows, width = weights.shape[1:]
    half = jax.ShapeDtypeStruct((count // 2, rows, width), jnp.bfloat16)
    return pl.pallas_call(
        functools.partial(renew_kernel, count),
        out_shape=(half, half),
        in_specs=[SMEM, ANY] + [VMEM] * len(backs),
        scratch_shapes=[
            pltpu.VMEM((count, rows, width), jnp.bfloat16),
            pltpu.SemaphoreType.DMA((count,)),
        ],
        compiler_params=SMALL,
    )(table, in_hbm(weights), *[in_vmem(x) for x in backs])


def pass_kernel(count, *refs):
    for ref, out in zip(refs[:count], refs[-count:]):
        for j in range(ref.shape[0]):
            out[j] = ref[j]


def pass_tables(tables, after=()):
    return pl.pallas_call(
        functools.partial(pass_kernel, len(tables)),
        out_shape=[jax.ShapeDtypeStruct(t.shape, t.dtype) for t in tables],
        in_specs=[SMEM] * len(tables) + [VMEM] * len(after),
        out_specs=[SMEM] * len(tables),
        compiler_params=SMALL,
    )(*tables, *[in_vmem(a) for a in after])


def scatter_kernel(place, *refs):
    pieces, out, sems = refs[:-2], refs[-2], refs[-1]
    copies = []
    for piece in pieces:
        for j in range(piece.shape[0]):
            n = len(copies)
            copies.append(pltpu.make_async_copy(piece.at[j], out.at[place[n]], sems.at[n]))
    for c in copies:
        c.start()
    for c in copies:
        c.wait()


def scatter_more_kernel(place, base, *refs):
    del base
    scatter_kernel(place, *refs)


def scatter_blocks(place, pieces, out_shape, base=None):
    pieces = [in_vmem(p) for p in pieces]
    count = sum(p.shape[0] for p in pieces)
    operands = pieces if base is None else [in_hbm(base)] + pieces
    return pl.pallas_call(
        scatter_kernel if base is None else scatter_more_kernel,
        out_shape=out_shape,
        in_specs=[SMEM] + [ANY] * (len(operands) - len(pieces)) + [pl.BlockSpec(memory_space=pltpu.VMEM)] * len(pieces),
        out_specs=ANY,
        scratch_shapes=[pltpu.SemaphoreType.DMA((count,))],
        input_output_aliases={} if base is None else {1: 0},
        compiler_params=SMALL,
    )(place, *operands)


def body(gradients, second_moment, inverse_roots, owners, weights):
    groups = lax.axis_size("groups")
    shards = lax.axis_size("shard")
    g = lax.axis_index("groups")
    total_blocks = owners.shape[0]
    nbg = total_blocks // groups
    slots = inverse_roots.shape[2]
    rows = gradients.shape[2]
    width = gradients.shape[3]
    half = nbg // 2

    def shift(n):
        return [(i, (i + n) % groups) for i in range(groups)]

    starts = [sum(CHUNKS[:c]) for c in range(len(CHUNKS))]
    received = []
    grads = gradients
    for start, per in zip(starts, CHUNKS):
        pieces = [
            lax.dynamic_slice(grads[0], (nbg * ((g + n) % groups), start, 0), (nbg, per, width)) for n in (1, 3, 2)
        ]
        grads, pieces = lax.optimization_barrier((grads, pieces))
        received.append([lax.ppermute(p, "groups", shift(n)) for p, n in zip(pieces, (1, 3, 2))])

    ids = jnp.arange(nbg, dtype=jnp.int32)
    earlier = ids[None, :] < ids[:, None]
    my_owner = lax.dynamic_slice_in_dim(owners, nbg * g, nbg)
    my_rank = jnp.sum(((my_owner[:, None] == my_owner[None, :]) & earlier).astype(jnp.int32), axis=1)
    meta = jnp.concatenate([g[None].astype(jnp.int32), my_owner, my_rank])
    grouped = owners.reshape(groups, nbg)
    same = grouped[:, :, None] == grouped[:, None, :]
    rank = jnp.sum((same & earlier[None]).astype(jnp.int32), axis=2)
    firsts = rank == 0
    before = jnp.sum((firsts[:, None, :] & earlier[None]).astype(jnp.int32), axis=2)
    n_first = jnp.sum(firsts.astype(jnp.int32), axis=1, keepdims=True)
    spot = jnp.where(firsts, before, n_first + ids[None] - before)
    sits = spot[:, None, :] == ids[None, :, None]
    order = jnp.sum(jnp.where(sits, ids[None, None, :], 0), axis=2)
    by_order = [
        lax.dynamic_index_in_dim(jnp.sum(jnp.where(sits, t[:, None, :], 0), axis=2), g, 0, False)
        for t in (jnp.broadcast_to(ids[None], grouped.shape), grouped, rank)
    ]

    def exchange(x, after=None):
        if after is not None:
            x, after = lax.optimization_barrier((x, after))
        return lax.all_to_all(x, "shard", 0, 0, tiled=True)

    columns = width + LANES
    norm = None
    coded = []
    for c in range(0, len(starts), 2):
        tall = CHUNKS[c] + CHUNKS[c + 1]
        final = c + 2 == len(starts)
        shapes = [(shards, tall, columns)] * slots if final else [(shards, slots, tall, columns)]
        code = []
        for d in (c, c + 1):
            last = final and d > c
            code = sum_replicas(
                gradients, received[d], second_moment, starts[d], meta, norm, last, starts[d] - starts[c], shapes, code
            )
            norm = None if last else code[-1]
            code = code[: len(shapes)]
        coded.append(code)
    early = exchange(coded[0][0])
    arrived = []
    for k in range(slots):
        arrived.append([early, exchange(coded[1][k], arrived[-1][-1] if k else early)])

    backs = []
    for k in range(slots):
        update = owner_work(inverse_roots, arrived[k], k)
        backs.append(exchange(update.reshape(shards, rows, width), backs[-1] if k else None))

    def to_all(new):
        a, b = new
        prev_a = lax.ppermute(a, "groups", shift(1))
        after_b = lax.ppermute(b, "groups", shift(3))
        prev_b = lax.ppermute(b, "groups", shift(1))
        after_a = lax.ppermute(a, "groups", shift(3))
        far_a = lax.ppermute(prev_a, "groups", shift(1))
        far_b = lax.ppermute(after_b, "groups", shift(3))
        return [a, b, prev_a, prev_b, after_a, after_b, far_a, far_b]

    def places(lo, hi):
        out = []
        for n in (0, 3, 1, 2):
            h = (g + n) % groups
            out.append(nbg * h + lax.dynamic_index_in_dim(order, h, 0, False)[lo:hi])
        return jnp.concatenate(out)

    def table(lo, hi):
        return jnp.concatenate([t[lo:hi] for t in by_order])

    out_shape = jax.ShapeDtypeStruct((total_blocks, rows, width), jnp.bfloat16)
    where = places(half, nbg)
    far = 3 * half
    tables = [table(0, half), table(half, nbg), places(0, half), where[:far], where[far:]]
    tables = pass_tables(tables)
    new = renew(tables[0], weights, backs[:1])
    pieces0 = to_all(new)
    late = pass_tables(tables[1:2], [pieces0[2], pieces0[5]])
    new = renew(late[0], weights, backs)
    pieces1 = to_all(new)
    out = scatter_blocks(tables[2], pieces0, out_shape)
    out = scatter_blocks(tables[3], pieces1[:6], out_shape, base=out)
    return scatter_blocks(tables[4], pieces1[6:], out_shape, base=out)


def solution(mesh):
    return jax.shard_map(
        body,
        mesh=mesh,
        in_specs=(
            P("groups", None, "shard", None),
            P("groups", "shard", None),
            P("groups", "shard", None, None, None, None),
            P(),
            P("groups", "shard", None),
        ),
        out_specs=P(None, "shard", None),
        check_vma=False,
    )
```

```python
import functools

import jax
import jax.numpy as jnp
from jax import lax
from jax.experimental import pallas as pl
from jax.experimental.pallas import tpu as pltpu
from jax.sharding import PartitionSpec as P


LANES = 128
CHUNKS = (8, 8, 8, 8)
TALL = 256
ANY = pl.BlockSpec(memory_space=pl.ANY)
SMEM = pl.BlockSpec(memory_space=pltpu.SMEM)
SMALL = pltpu.CompilerParams(vmem_limit_bytes=12 * 2**20)
LARGE = pltpu.CompilerParams(vmem_limit_bytes=20 * 2**20)
VMEM = pl.BlockSpec(memory_space=pltpu.VMEM)


def in_hbm(x):
    return pltpu.with_memory_space_constraint(x, pltpu.HBM)


def in_vmem(x):
    return pltpu.with_memory_space_constraint(x, pltpu.VMEM)


def two_parts(values):
    high = values.astype(jnp.bfloat16)
    low = (values - high.astype(jnp.float32)).astype(jnp.bfloat16)
    return high, low


def dot(a, b):
    return jnp.dot(a, b, preferred_element_type=jnp.float32)


def sum_kernel(start, offset, first, last, n_base, meta, gradients, one, two, three, old_all, *refs):
    before = None if first else refs[0]
    outs = refs[(0 if first else 1) + n_base : -5]
    norms = None if last else outs[-1]
    outs = outs if last else outs[:-1]
    own, old, codes, in_sems, sems = refs[-5:]
    nbg, per, width = one.shape
    rows = pl.ds(start, per)
    loads = [
        pltpu.make_async_copy(gradients.at[0, pl.ds(meta[0] * nbg, nbg), rows], own, in_sems.at[0]),
        pltpu.make_async_copy(old_all.at[:, rows], old, in_sems.at[1]),
    ]
    for x in loads:
        x.start()
    for x in loads:
        x.wait()

    def code_block(at):
        total = (own[at].astype(jnp.float32) + one[at].astype(jnp.float32)) + (
            two[at].astype(jnp.float32) + three[at].astype(jnp.float32)
        )
        moment = 0.95 * old[at].astype(jnp.float32) + 0.05 * total * total
        adam = total / (moment * lax.rsqrt(moment) + 1e-08)
        adam = adam * adam
        parts = [total[:, j : j + LANES] for j in range(0, width, LANES)]
        top = functools.reduce(jnp.maximum, [jnp.abs(p) for p in parts])
        if last:
            top = jnp.maximum(top, pltpu.roll(top, 4, 0))
        power = jnp.floor(jnp.log2(jnp.maximum(top, 1e-30)) + 1e-4) - 14.0
        grow = jnp.exp2(-power)
        for j, p in enumerate(parts):
            codes[at, :, j * LANES : (j + 1) * LANES] = jnp.round(p * grow).astype(jnp.int32).astype(jnp.int16)
        squares = functools.reduce(jnp.add, [adam[:, j : j + LANES] for j in range(0, width, LANES)])
        squares = jnp.sum(squares, axis=0, keepdims=True)
        if not first:
            squares = squares + before[at]
        if not last:
            norms[at] = squares
            codes[at, :, width:] = power.astype(jnp.int32).astype(jnp.int16)
            return
        scale = jnp.ceil(jnp.log2(jnp.maximum(squares, 1e-30)))
        scaled = squares * jnp.exp2(14.0 - scale)
        high = jnp.floor(scaled)
        low = jnp.floor((scaled - high) * 16384.0)
        row = lax.broadcasted_iota(jnp.int32, power.shape, 0)
        full = jnp.where(row < 4, power, jnp.where(row == 4, scale, jnp.where(row == 5, high, low)))
        codes[at, :, width:] = full.astype(jnp.int32).astype(jnp.int16)

    def block(at, _):
        code_block(at)
        owner, rank = meta[1 + at], meta[1 + nbg + at]
        if len(outs) == 1:
            to = outs[0].at[owner, jnp.minimum(rank, outs[0].shape[1] - 1), to_rows]
            pltpu.make_async_copy(codes.at[at], to, sems.at[at]).start()
        else:
            for k, out in enumerate(outs):

                @pl.when(rank == k)
                def _():
                    pltpu.make_async_copy(codes.at[at], out.at[owner, to_rows], sems.at[at]).start()

        return 0

    to_rows = pl.ds(offset, per)
    lax.fori_loop(0, nbg, block, 0)
    done = outs[0].at[0, 0, to_rows] if len(outs) == 1 else outs[0].at[0, to_rows]
    for n in range(nbg):
        pltpu.make_async_copy(codes.at[n], done, sems.at[n]).wait()


def sum_replicas(gradients, received, old, start, meta, before, last, offset, shapes, base):
    nbg, per, width = received[0].shape
    columns = width + LANES
    out_shapes = [pltpu.HBM(x, jnp.int16) for x in shapes]
    if not last:
        out_shapes.append(jax.ShapeDtypeStruct((nbg, 1, LANES), jnp.float32))
    carried = [] if before is None else [before]
    base = [in_hbm(x) for x in base]
    return pl.pallas_call(
        functools.partial(sum_kernel, start, offset, before is None, last, len(base)),
        out_shape=out_shapes,
        in_specs=[SMEM, ANY, VMEM, VMEM, VMEM, ANY] + [VMEM] * len(carried) + [ANY] * len(base),
        out_specs=[ANY] * len(shapes) + ([] if last else [VMEM]),
        scratch_shapes=[
            pltpu.VMEM((nbg, per, width), jnp.bfloat16),
            pltpu.VMEM((nbg, per, width), jnp.bfloat16),
            pltpu.VMEM((nbg, per, columns), jnp.int16),
            pltpu.SemaphoreType.DMA((2,)),
            pltpu.SemaphoreType.DMA((nbg,)),
        ],
        input_output_aliases={6 + len(carried) + n: n for n in range(len(base))},
        compiler_params=SMALL,
    )(meta, in_hbm(gradients), *[in_vmem(r) for r in received], in_hbm(old), *carried, *base)


def owner_kernel(slot, all_roots, *refs):
    early, late, out, high, low, pre, roots, update, sems, out_sems = refs
    width = update.shape[0]
    loads = [pltpu.make_async_copy(all_roots.at[0, 0, slot, k], roots.at[k], sems.at[k]) for k in (1, 0)]
    for x in loads:
        x.start()
    n_src, per = late.shape[:2]
    rows = 2 * per

    def unpack(n, graft):
        codes = [early[n, slot], late[n]]
        tails = [x[:, width:].astype(jnp.int32).astype(jnp.float32) for x in codes]
        norm = tails[1][8:]
        row = lax.broadcasted_iota(jnp.int32, norm.shape, 0)
        tails[1] = jnp.concatenate([tails[1][:8], jnp.where(row < 4, norm, pltpu.roll(norm, 4, 0))], axis=0)
        for c, (code, tail) in enumerate(zip(codes, tails)):
            at = pl.ds(pl.multiple_of(n * rows + c * per, per), per)
            step = jnp.exp2(tail)
            for j in range(0, width, LANES):
                value = code[:, j : j + LANES].astype(jnp.int32).astype(jnp.float32) * step
                high[at, j : j + LANES], low[at, j : j + LANES] = two_parts(value)
        return graft + jnp.exp2(norm[4:5] - 14.0) * (norm[5:6] + norm[6:7] * (1.0 / 16384.0))

    graft = lax.fori_loop(0, n_src, unpack, jnp.zeros((1, LANES), jnp.float32))
    graft = jnp.sum(graft, axis=1, keepdims=True)
    loads[0].wait()
    right = roots[1]
    for m in range(0, width, TALL):
        at = pl.ds(m, TALL)
        high[at, :], low[at, :] = two_parts(dot(high[at, :], right) + dot(low[at, :], right))
    loads[1].wait()
    square = jnp.zeros((1, width), jnp.float32)
    for m in range(0, width, TALL):
        at = pl.ds(m, TALL)
        left = roots[0, at, :]
        got = dot(left, high[...]) + dot(left, low[...])
        pre[at, :] = got
        square = square + jnp.sum(got * got, axis=0, keepdims=True)
    square = jnp.sum(square, axis=1, keepdims=True)
    scale = jnp.sqrt(graft) / jnp.sqrt(square + 1e-06)
    copies = []
    for n, m in enumerate(range(0, width, TALL)):
        at = pl.ds(m, TALL)
        update[at, :] = (scale * pre[at, :]).astype(jnp.bfloat16)
        copies.append(pltpu.make_async_copy(update.at[at], out.at[at], out_sems.at[n]))
        copies[-1].start()
    for c in copies:
        c.wait()


def owner_work(roots, arrived, slot):
    width = roots.shape[-1]
    return pl.pallas_call(
        functools.partial(owner_kernel, slot),
        out_shape=pltpu.HBM((width, width), jnp.bfloat16),
        in_specs=[ANY] + [VMEM] * len(arrived),
        out_specs=ANY,
        scratch_shapes=[
            pltpu.VMEM((width, width), jnp.bfloat16),
            pltpu.VMEM((width, width), jnp.bfloat16),
            pltpu.VMEM((width, width), jnp.float32),
            pltpu.VMEM((2, width, width), jnp.bfloat16),
            pltpu.VMEM((width, width), jnp.bfloat16),
            pltpu.SemaphoreType.DMA((2,)),
            pltpu.SemaphoreType.DMA((width // TALL,)),
        ],
        compiler_params=LARGE,
    )(in_hbm(roots), *[in_vmem(a) for a in arrived])


def order_kernel(table, weights, out, sems):
    copies = [pltpu.make_async_copy(weights.at[table[j]], out.at[j], sems.at[j]) for j in range(out.shape[0])]
    for c in copies:
        c.start()
    for c in copies:
        c.wait()


def order_blocks(table, weights):
    count = table.shape[0]
    return pl.pallas_call(
        order_kernel,
        out_shape=pltpu.VMEM((count,) + weights.shape[1:], weights.dtype),
        in_specs=[SMEM, ANY],
        out_specs=VMEM,
        scratch_shapes=[pltpu.SemaphoreType.DMA((count,))],
        compiler_params=SMALL,
    )(table, in_hbm(weights))


def renew_kernel(first, table, weights, *refs):
    backs, outs = refs[:-2], refs[-2:]
    half = outs[0].shape[0]

    def block(j, k):
        grad = backs[k][table[j]].astype(jnp.float32)
        stepped = weights[first + j].astype(jnp.float32) - 0.5 * grad
        scale = lax.rsqrt(jnp.mean(stepped * stepped, axis=1, keepdims=True) + 1e-06)
        outs[j // half][j % half] = (stepped * scale).astype(jnp.bfloat16)

    for j in range(2 * half):
        if len(backs) == 1:
            block(j, 0)
            continue
        for k in range(len(backs)):
            pl.when(table[2 * half + j] == k)(functools.partial(block, j, k))


def renew(table, weights, backs, first):
    count = table.shape[0] // 2
    half = pltpu.VMEM((count // 2,) + weights.shape[1:], jnp.bfloat16)
    return pl.pallas_call(
        functools.partial(renew_kernel, first),
        out_shape=(half, half),
        in_specs=[SMEM] + [VMEM] * (1 + len(backs)),
        out_specs=(VMEM, VMEM),
        compiler_params=SMALL,
    )(table, in_vmem(weights), *[in_vmem(x) for x in backs])


def pass_kernel(count, *refs):
    for ref, out in zip(refs[:count], refs[-count:]):
        for j in range(ref.shape[0]):
            out[j] = ref[j]


def pass_tables(tables, after=()):
    return pl.pallas_call(
        functools.partial(pass_kernel, len(tables)),
        out_shape=[jax.ShapeDtypeStruct(t.shape, t.dtype) for t in tables],
        in_specs=[SMEM] * len(tables) + [VMEM] * len(after),
        out_specs=[SMEM] * len(tables),
        compiler_params=SMALL,
    )(*tables, *[in_vmem(a) for a in after])


def scatter_kernel(place, *refs):
    pieces, out, sems = refs[:-2], refs[-2], refs[-1]
    copies = []
    for piece in pieces:
        for j in range(piece.shape[0]):
            n = len(copies)
            copies.append(pltpu.make_async_copy(piece.at[j], out.at[place[n]], sems.at[n]))
    for c in copies:
        c.start()
    for c in copies:
        c.wait()


def scatter_more_kernel(place, base, *refs):
    del base
    scatter_kernel(place, *refs)


def scatter_blocks(place, pieces, out_shape, base=None):
    pieces = [in_vmem(p) for p in pieces]
    count = sum(p.shape[0] for p in pieces)
    operands = pieces if base is None else [in_hbm(base)] + pieces
    return pl.pallas_call(
        scatter_kernel if base is None else scatter_more_kernel,
        out_shape=out_shape,
        in_specs=[SMEM] + [ANY] * (len(operands) - len(pieces)) + [pl.BlockSpec(memory_space=pltpu.VMEM)] * len(pieces),
        out_specs=ANY,
        scratch_shapes=[pltpu.SemaphoreType.DMA((count,))],
        input_output_aliases={} if base is None else {1: 0},
        compiler_params=SMALL,
    )(place, *operands)


def body(gradients, second_moment, inverse_roots, owners, weights):
    groups = lax.axis_size("groups")
    shards = lax.axis_size("shard")
    g = lax.axis_index("groups")
    total_blocks = owners.shape[0]
    nbg = total_blocks // groups
    slots = inverse_roots.shape[2]
    rows = gradients.shape[2]
    width = gradients.shape[3]
    half = nbg // 2

    def shift(n):
        return [(i, (i + n) % groups) for i in range(groups)]

    starts = [sum(CHUNKS[:c]) for c in range(len(CHUNKS))]
    received = []
    grads = gradients
    for start, per in zip(starts, CHUNKS):
        pieces = [
            lax.dynamic_slice(grads[0], (nbg * ((g + n) % groups), start, 0), (nbg, per, width)) for n in (1, 3, 2)
        ]
        grads, pieces = lax.optimization_barrier((grads, pieces))
        received.append([lax.ppermute(p, "groups", shift(n)) for p, n in zip(pieces, (1, 3, 2))])

    ids = jnp.arange(nbg, dtype=jnp.int32)
    earlier = ids[None, :] < ids[:, None]
    my_owner = lax.dynamic_slice_in_dim(owners, nbg * g, nbg)
    my_rank = jnp.sum(((my_owner[:, None] == my_owner[None, :]) & earlier).astype(jnp.int32), axis=1)
    meta = jnp.concatenate([g[None].astype(jnp.int32), my_owner, my_rank])
    grouped = owners.reshape(groups, nbg)
    same = grouped[:, :, None] == grouped[:, None, :]
    rank = jnp.sum((same & earlier[None]).astype(jnp.int32), axis=2)
    firsts = rank == 0
    before = jnp.sum((firsts[:, None, :] & earlier[None]).astype(jnp.int32), axis=2)
    n_first = jnp.sum(firsts.astype(jnp.int32), axis=1, keepdims=True)
    spot = jnp.where(firsts, before, n_first + ids[None] - before)
    sits = spot[:, None, :] == ids[None, :, None]
    order = jnp.sum(jnp.where(sits, ids[None, None, :], 0), axis=2)
    by_order = [
        lax.dynamic_index_in_dim(jnp.sum(jnp.where(sits, t[:, None, :], 0), axis=2), g, 0, False)
        for t in (jnp.broadcast_to(ids[None], grouped.shape), grouped, rank)
    ]

    def exchange(x, after=None):
        if after is not None:
            x, after = lax.optimization_barrier((x, after))
        return lax.all_to_all(x, "shard", 0, 0, tiled=True)

    columns = width + LANES
    norm = None
    coded = []
    for c in range(0, len(starts), 2):
        tall = CHUNKS[c] + CHUNKS[c + 1]
        final = c + 2 == len(starts)
        shapes = [(shards, tall, columns)] * slots if final else [(shards, slots, tall, columns)]
        code = []
        for d in (c, c + 1):
            last = final and d > c
            code = sum_replicas(
                gradients, received[d], second_moment, starts[d], meta, norm, last, starts[d] - starts[c], shapes, code
            )
            norm = None if last else code[-1]
            code = code[: len(shapes)]
        coded.append(code)
    early = exchange(coded[0][0])
    arrived = []
    for k in range(slots):
        arrived.append([early, exchange(coded[1][k], arrived[-1][-1] if k else early)])

    backs = []
    for k in range(slots):
        update = owner_work(inverse_roots, arrived[k], k)
        backs.append(exchange(update.reshape(shards, rows, width), backs[-1] if k else None))

    def to_all(new):
        a, b = new
        prev_a = lax.ppermute(a, "groups", shift(1))
        after_b = lax.ppermute(b, "groups", shift(3))
        prev_b = lax.ppermute(b, "groups", shift(1))
        after_a = lax.ppermute(a, "groups", shift(3))
        far_a = lax.ppermute(prev_a, "groups", shift(1))
        far_b = lax.ppermute(after_b, "groups", shift(3))
        return [a, b, prev_a, prev_b, after_a, after_b, far_a, far_b]

    def places(lo, hi):
        out = []
        for n in (0, 3, 1, 2):
            h = (g + n) % groups
            out.append(nbg * h + lax.dynamic_index_in_dim(order, h, 0, False)[lo:hi])
        return jnp.concatenate(out)

    def table(lo, hi):
        return jnp.concatenate([t[lo:hi] for t in by_order[1:]])

    out_shape = jax.ShapeDtypeStruct((total_blocks, rows, width), jnp.bfloat16)
    where = places(half, nbg)
    far = 3 * half
    tables = [table(0, half), table(half, nbg), places(0, half), where[:far], where[far:], by_order[0]]
    tables = pass_tables(tables)
    ordered = order_blocks(tables[5], weights)
    new = renew(tables[0], ordered, backs[:1], 0)
    pieces0 = to_all(new)
    late = pass_tables(tables[1:2], [pieces0[2], pieces0[5]])
    new = renew(late[0], ordered, backs, half)
    pieces1 = to_all(new)
    out = scatter_blocks(tables[2], pieces0, out_shape)
    out = scatter_blocks(tables[3], pieces1[:6], out_shape, base=out)
    return scatter_blocks(tables[4], pieces1[6:], out_shape, base=out)


def solution(mesh):
    return jax.shard_map(
        body,
        mesh=mesh,
        in_specs=(
            P("groups", None, "shard", None),
            P("groups", "shard", None),
            P("groups", "shard", None, None, None, None),
            P(),
            P("groups", "shard", None),
        ),
        out_specs=P(None, "shard", None),
        check_vma=False,
    )
```

```python
import functools

import jax
import jax.numpy as jnp
from jax import lax
from jax.experimental import pallas as pl
from jax.experimental.pallas import tpu as pltpu
from jax.sharding import PartitionSpec as P


LANES = 128
CHUNKS = (8, 8, 8, 8)
TALL = 256
ANY = pl.BlockSpec(memory_space=pl.ANY)
SMEM = pl.BlockSpec(memory_space=pltpu.SMEM)
SMALL = pltpu.CompilerParams(vmem_limit_bytes=12 * 2**20)
LARGE = pltpu.CompilerParams(vmem_limit_bytes=20 * 2**20)
VMEM = pl.BlockSpec(memory_space=pltpu.VMEM)


def in_hbm(x):
    return pltpu.with_memory_space_constraint(x, pltpu.HBM)


def in_vmem(x):
    return pltpu.with_memory_space_constraint(x, pltpu.VMEM)


def two_parts(values):
    high = values.astype(jnp.bfloat16)
    low = (values - high.astype(jnp.float32)).astype(jnp.bfloat16)
    return high, low


def dot(a, b):
    return jnp.dot(a, b, preferred_element_type=jnp.float32)


def sum_kernel(start, offset, first, last, n_base, meta, gradients, one, two, three, old_all, *refs):
    before = None if first else refs[0]
    outs = refs[(0 if first else 1) + n_base : -5]
    norms = None if last else outs[-1]
    outs = outs if last else outs[:-1]
    own, old, codes, in_sems, sems = refs[-5:]
    nbg, per, width = one.shape
    rows = pl.ds(start, per)
    loads = [
        pltpu.make_async_copy(gradients.at[0, pl.ds(meta[0] * nbg, nbg), rows], own, in_sems.at[0]),
        pltpu.make_async_copy(old_all.at[:, rows], old, in_sems.at[1]),
    ]
    for x in loads:
        x.start()
    for x in loads:
        x.wait()

    def code_block(at):
        total = (own[at].astype(jnp.float32) + one[at].astype(jnp.float32)) + (
            two[at].astype(jnp.float32) + three[at].astype(jnp.float32)
        )
        moment = 0.95 * old[at].astype(jnp.float32) + 0.05 * total * total
        adam = total / (moment * lax.rsqrt(moment) + 1e-08)
        adam = adam * adam
        parts = [total[:, j : j + LANES] for j in range(0, width, LANES)]
        top = functools.reduce(jnp.maximum, [jnp.abs(p) for p in parts])
        if last:
            top = jnp.maximum(top, pltpu.roll(top, 4, 0))
        power = jnp.floor(jnp.log2(jnp.maximum(top, 1e-30)) + 1e-4) - 14.0
        grow = jnp.exp2(-power)
        for j, p in enumerate(parts):
            codes[at, :, j * LANES : (j + 1) * LANES] = jnp.round(p * grow).astype(jnp.int32).astype(jnp.int16)
        squares = functools.reduce(jnp.add, [adam[:, j : j + LANES] for j in range(0, width, LANES)])
        squares = jnp.sum(squares, axis=0, keepdims=True)
        if not first:
            squares = squares + before[at]
        if not last:
            norms[at] = squares
            codes[at, :, width:] = power.astype(jnp.int32).astype(jnp.int16)
            return
        scale = jnp.ceil(jnp.log2(jnp.maximum(squares, 1e-30)))
        scaled = squares * jnp.exp2(14.0 - scale)
        high = jnp.floor(scaled)
        low = jnp.floor((scaled - high) * 16384.0)
        row = lax.broadcasted_iota(jnp.int32, power.shape, 0)
        full = jnp.where(row < 4, power, jnp.where(row == 4, scale, jnp.where(row == 5, high, low)))
        codes[at, :, width:] = full.astype(jnp.int32).astype(jnp.int16)

    def block(at, _):
        code_block(at)
        owner, rank = meta[1 + at], meta[1 + nbg + at]
        if len(outs) == 1:
            to = outs[0].at[owner, jnp.minimum(rank, outs[0].shape[1] - 1), to_rows]
            pltpu.make_async_copy(codes.at[at], to, sems.at[at]).start()
        else:
            for k, out in enumerate(outs):

                @pl.when(rank == k)
                def _():
                    pltpu.make_async_copy(codes.at[at], out.at[owner, to_rows], sems.at[at]).start()

        return 0

    to_rows = pl.ds(offset, per)
    lax.fori_loop(0, nbg, block, 0)
    done = outs[0].at[0, 0, to_rows] if len(outs) == 1 else outs[0].at[0, to_rows]
    for n in range(nbg):
        pltpu.make_async_copy(codes.at[n], done, sems.at[n]).wait()


def sum_replicas(gradients, received, old, start, meta, before, last, offset, shapes, base):
    nbg, per, width = received[0].shape
    columns = width + LANES
    out_shapes = [pltpu.HBM(x, jnp.int16) for x in shapes]
    if not last:
        out_shapes.append(jax.ShapeDtypeStruct((nbg, 1, LANES), jnp.float32))
    carried = [] if before is None else [before]
    base = [in_hbm(x) for x in base]
    return pl.pallas_call(
        functools.partial(sum_kernel, start, offset, before is None, last, len(base)),
        out_shape=out_shapes,
        in_specs=[SMEM, ANY, VMEM, VMEM, VMEM, ANY] + [VMEM] * len(carried) + [ANY] * len(base),
        out_specs=[ANY] * len(shapes) + ([] if last else [VMEM]),
        scratch_shapes=[
            pltpu.VMEM((nbg, per, width), jnp.bfloat16),
            pltpu.VMEM((nbg, per, width), jnp.bfloat16),
            pltpu.VMEM((nbg, per, columns), jnp.int16),
            pltpu.SemaphoreType.DMA((2,)),
            pltpu.SemaphoreType.DMA((nbg,)),
        ],
        input_output_aliases={6 + len(carried) + n: n for n in range(len(base))},
        compiler_params=SMALL,
    )(meta, in_hbm(gradients), *[in_vmem(r) for r in received], in_hbm(old), *carried, *base)


def owner_kernel(slot, all_roots, *refs):
    early, late, out, high, low, pre, roots, update, sems, out_sems = refs
    width = update.shape[0]
    loads = [pltpu.make_async_copy(all_roots.at[0, 0, slot, k], roots.at[k], sems.at[k]) for k in (1, 0)]
    for x in loads:
        x.start()
    n_src, per = late.shape[:2]
    rows = 2 * per

    def unpack(n, graft):
        codes = [early[n, slot], late[n]]
        tails = [x[:, width:].astype(jnp.int32).astype(jnp.float32) for x in codes]
        norm = tails[1][8:]
        row = lax.broadcasted_iota(jnp.int32, norm.shape, 0)
        tails[1] = jnp.concatenate([tails[1][:8], jnp.where(row < 4, norm, pltpu.roll(norm, 4, 0))], axis=0)
        for c, (code, tail) in enumerate(zip(codes, tails)):
            at = pl.ds(pl.multiple_of(n * rows + c * per, per), per)
            step = jnp.exp2(tail)
            for j in range(0, width, LANES):
                value = code[:, j : j + LANES].astype(jnp.int32).astype(jnp.float32) * step
                high[at, j : j + LANES], low[at, j : j + LANES] = two_parts(value)
        return graft + jnp.exp2(norm[4:5] - 14.0) * (norm[5:6] + norm[6:7] * (1.0 / 16384.0))

    graft = lax.fori_loop(0, n_src, unpack, jnp.zeros((1, LANES), jnp.float32))
    graft = jnp.sum(graft, axis=1, keepdims=True)
    loads[0].wait()
    right = roots[1]
    for m in range(0, width, TALL):
        at = pl.ds(m, TALL)
        high[at, :], low[at, :] = two_parts(dot(high[at, :], right) + dot(low[at, :], right))
    loads[1].wait()
    square = jnp.zeros((1, width), jnp.float32)
    for m in range(0, width, TALL):
        at = pl.ds(m, TALL)
        left = roots[0, at, :]
        got = dot(left, high[...]) + dot(left, low[...])
        pre[at, :] = got
        square = square + jnp.sum(got * got, axis=0, keepdims=True)
    square = jnp.sum(square, axis=1, keepdims=True)
    scale = jnp.sqrt(graft) / jnp.sqrt(square + 1e-06)
    copies = []
    for n, m in enumerate(range(0, width, TALL)):
        at = pl.ds(m, TALL)
        update[at, :] = (scale * pre[at, :]).astype(jnp.bfloat16)
        copies.append(pltpu.make_async_copy(update.at[at], out.at[at], out_sems.at[n]))
        copies[-1].start()
    for c in copies:
        c.wait()


def owner_work(roots, arrived, slot):
    width = roots.shape[-1]
    return pl.pallas_call(
        functools.partial(owner_kernel, slot),
        out_shape=pltpu.HBM((width, width), jnp.bfloat16),
        in_specs=[ANY] + [VMEM] * len(arrived),
        out_specs=ANY,
        scratch_shapes=[
            pltpu.VMEM((width, width), jnp.bfloat16),
            pltpu.VMEM((width, width), jnp.bfloat16),
            pltpu.VMEM((width, width), jnp.float32),
            pltpu.VMEM((2, width, width), jnp.bfloat16),
            pltpu.VMEM((width, width), jnp.bfloat16),
            pltpu.SemaphoreType.DMA((2,)),
            pltpu.SemaphoreType.DMA((width // TALL,)),
        ],
        compiler_params=LARGE,
    )(in_hbm(roots), *[in_vmem(a) for a in arrived])


def order_kernel(table, weights, out, sems):
    copies = [pltpu.make_async_copy(weights.at[table[j]], out.at[j], sems.at[j]) for j in range(out.shape[0])]
    for c in copies:
        c.start()
    for c in copies:
        c.wait()


def order_blocks(table, weights):
    count = table.shape[0]
    return pl.pallas_call(
        order_kernel,
        out_shape=pltpu.VMEM((count,) + weights.shape[1:], weights.dtype),
        in_specs=[SMEM, ANY],
        out_specs=VMEM,
        scratch_shapes=[pltpu.SemaphoreType.DMA((count,))],
        compiler_params=SMALL,
    )(table, in_hbm(weights))


def renew_kernel(first, slot, table, weights, back, *refs):
    outs = refs[-2:]
    made = refs[:-2]
    half = outs[0].shape[0]

    def block(j):
        grad = back[table[j]].astype(jnp.float32)
        stepped = weights[first + j].astype(jnp.float32) - 0.5 * grad
        scale = lax.rsqrt(jnp.mean(stepped * stepped, axis=1, keepdims=True) + 1e-06)
        outs[j // half][j % half] = (stepped * scale).astype(jnp.bfloat16)

    def keep(j):
        outs[j // half][j % half] = made[j // half][j % half]

    for j in range(2 * half):
        if not made:
            block(j)
            continue
        pl.when(table[2 * half + j] == slot)(functools.partial(block, j))
        pl.when(table[2 * half + j] != slot)(functools.partial(keep, j))


def renew(table, weights, back, first, slot, made=()):
    count = table.shape[0] // 2
    half = pltpu.VMEM((count // 2,) + weights.shape[1:], jnp.bfloat16)
    return pl.pallas_call(
        functools.partial(renew_kernel, first, slot),
        out_shape=(half, half),
        in_specs=[SMEM] + [VMEM] * (2 + len(made)),
        out_specs=(VMEM, VMEM),
        compiler_params=SMALL,
    )(table, in_vmem(weights), in_vmem(back), *[in_vmem(x) for x in made])


def pass_kernel(count, *refs):
    for ref, out in zip(refs[:count], refs[-count:]):
        for j in range(ref.shape[0]):
            out[j] = ref[j]


def pass_tables(tables, after=()):
    return pl.pallas_call(
        functools.partial(pass_kernel, len(tables)),
        out_shape=[jax.ShapeDtypeStruct(t.shape, t.dtype) for t in tables],
        in_specs=[SMEM] * len(tables) + [VMEM] * len(after),
        out_specs=[SMEM] * len(tables),
        compiler_params=SMALL,
    )(*tables, *[in_vmem(a) for a in after])


def scatter_kernel(place, *refs):
    pieces, out, sems = refs[:-2], refs[-2], refs[-1]
    copies = []
    for piece in pieces:
        for j in range(piece.shape[0]):
            n = len(copies)
            copies.append(pltpu.make_async_copy(piece.at[j], out.at[place[n]], sems.at[n]))
    for c in copies:
        c.start()
    for c in copies:
        c.wait()


def scatter_more_kernel(place, base, *refs):
    del base
    scatter_kernel(place, *refs)


def scatter_blocks(place, pieces, out_shape, base=None):
    pieces = [in_vmem(p) for p in pieces]
    count = sum(p.shape[0] for p in pieces)
    operands = pieces if base is None else [in_hbm(base)] + pieces
    return pl.pallas_call(
        scatter_kernel if base is None else scatter_more_kernel,
        out_shape=out_shape,
        in_specs=[SMEM] + [ANY] * (len(operands) - len(pieces)) + [pl.BlockSpec(memory_space=pltpu.VMEM)] * len(pieces),
        out_specs=ANY,
        scratch_shapes=[pltpu.SemaphoreType.DMA((count,))],
        input_output_aliases={} if base is None else {1: 0},
        compiler_params=SMALL,
    )(place, *operands)


def body(gradients, second_moment, inverse_roots, owners, weights):
    groups = lax.axis_size("groups")
    shards = lax.axis_size("shard")
    g = lax.axis_index("groups")
    total_blocks = owners.shape[0]
    nbg = total_blocks // groups
    slots = inverse_roots.shape[2]
    rows = gradients.shape[2]
    width = gradients.shape[3]
    half = nbg // 2

    def shift(n):
        return [(i, (i + n) % groups) for i in range(groups)]

    starts = [sum(CHUNKS[:c]) for c in range(len(CHUNKS))]
    received = []
    grads = gradients
    for start, per in zip(starts, CHUNKS):
        pieces = [
            lax.dynamic_slice(grads[0], (nbg * ((g + n) % groups), start, 0), (nbg, per, width)) for n in (1, 3, 2)
        ]
        grads, pieces = lax.optimization_barrier((grads, pieces))
        received.append([lax.ppermute(p, "groups", shift(n)) for p, n in zip(pieces, (1, 3, 2))])

    ids = jnp.arange(nbg, dtype=jnp.int32)
    earlier = ids[None, :] < ids[:, None]
    my_owner = lax.dynamic_slice_in_dim(owners, nbg * g, nbg)
    my_rank = jnp.sum(((my_owner[:, None] == my_owner[None, :]) & earlier).astype(jnp.int32), axis=1)
    meta = jnp.concatenate([g[None].astype(jnp.int32), my_owner, my_rank])
    grouped = owners.reshape(groups, nbg)
    same = grouped[:, :, None] == grouped[:, None, :]
    rank = jnp.sum((same & earlier[None]).astype(jnp.int32), axis=2)
    firsts = rank == 0
    before = jnp.sum((firsts[:, None, :] & earlier[None]).astype(jnp.int32), axis=2)
    n_first = jnp.sum(firsts.astype(jnp.int32), axis=1, keepdims=True)
    spot = jnp.where(firsts, before, n_first + ids[None] - before)
    sits = spot[:, None, :] == ids[None, :, None]
    order = jnp.sum(jnp.where(sits, ids[None, None, :], 0), axis=2)
    by_order = [
        lax.dynamic_index_in_dim(jnp.sum(jnp.where(sits, t[:, None, :], 0), axis=2), g, 0, False)
        for t in (jnp.broadcast_to(ids[None], grouped.shape), grouped, rank)
    ]

    def exchange(x, after=None):
        if after is not None:
            x, after = lax.optimization_barrier((x, after))
        return lax.all_to_all(x, "shard", 0, 0, tiled=True)

    columns = width + LANES
    norm = None
    coded = []
    for c in range(0, len(starts), 2):
        tall = CHUNKS[c] + CHUNKS[c + 1]
        final = c + 2 == len(starts)
        shapes = [(shards, tall, columns)] * slots if final else [(shards, slots, tall, columns)]
        code = []
        for d in (c, c + 1):
            last = final and d > c
            code = sum_replicas(
                gradients, received[d], second_moment, starts[d], meta, norm, last, starts[d] - starts[c], shapes, code
            )
            norm = None if last else code[-1]
            code = code[: len(shapes)]
        coded.append(code)
    early = exchange(coded[0][0])
    arrived = []
    for k in range(slots):
        arrived.append([early, exchange(coded[1][k], arrived[-1][-1] if k else early)])

    backs = []
    for k in range(slots):
        update = owner_work(inverse_roots, arrived[k], k)
        backs.append(exchange(update.reshape(shards, rows, width), backs[-1] if k else None))

    def to_all(new):
        a, b = new
        prev_a = lax.ppermute(a, "groups", shift(1))
        after_b = lax.ppermute(b, "groups", shift(3))
        prev_b = lax.ppermute(b, "groups", shift(1))
        after_a = lax.ppermute(a, "groups", shift(3))
        far_a = lax.ppermute(prev_a, "groups", shift(1))
        far_b = lax.ppermute(after_b, "groups", shift(3))
        return [a, b, prev_a, prev_b, after_a, after_b, far_a, far_b]

    def places(lo, hi):
        out = []
        for n in (0, 3, 1, 2):
            h = (g + n) % groups
            out.append(nbg * h + lax.dynamic_index_in_dim(order, h, 0, False)[lo:hi])
        return jnp.concatenate(out)

    def table(lo, hi):
        return jnp.concatenate([t[lo:hi] for t in by_order[1:]])

    out_shape = jax.ShapeDtypeStruct((total_blocks, rows, width), jnp.bfloat16)
    where = places(half, nbg)
    far = 3 * half
    tables = [table(0, half), table(half, nbg), places(0, half), where[:far], where[far:], by_order[0]]
    tables = pass_tables(tables)
    ordered = order_blocks(tables[5], weights)
    new = renew(tables[0], ordered, backs[0], 0, 0)
    pieces0 = to_all(new)
    late = pass_tables(tables[1:2], [pieces0[2], pieces0[5]])
    made = renew(late[0], ordered, backs[0], half, 0)
    new = renew(late[0], ordered, backs[1], half, 1, made)
    pieces1 = to_all(new)
    out = scatter_blocks(tables[2], pieces0, out_shape)
    out = scatter_blocks(tables[3], pieces1[:6], out_shape, base=out)
    return scatter_blocks(tables[4], pieces1[6:], out_shape, base=out)


def solution(mesh):
    return jax.shard_map(
        body,
        mesh=mesh,
        in_specs=(
            P("groups", None, "shard", None),
            P("groups", "shard", None),
            P("groups", "shard", None, None, None, None),
            P(),
            P("groups", "shard", None),
        ),
        out_specs=P(None, "shard", None),
        check_vma=False,
    )
```

```python
import functools

import jax
import jax.numpy as jnp
from jax import lax
from jax.experimental import pallas as pl
from jax.experimental.pallas import tpu as pltpu
from jax.sharding import PartitionSpec as P


LANES = 128
CHUNKS = (8, 8, 8, 8)
TALL = 256
ANY = pl.BlockSpec(memory_space=pl.ANY)
SMEM = pl.BlockSpec(memory_space=pltpu.SMEM)
SMALL = pltpu.CompilerParams(vmem_limit_bytes=12 * 2**20)
LARGE = pltpu.CompilerParams(vmem_limit_bytes=20 * 2**20)
VMEM = pl.BlockSpec(memory_space=pltpu.VMEM)


def in_hbm(x):
    return pltpu.with_memory_space_constraint(x, pltpu.HBM)


def in_vmem(x):
    return pltpu.with_memory_space_constraint(x, pltpu.VMEM)


def two_parts(values):
    high = values.astype(jnp.bfloat16)
    low = (values - high.astype(jnp.float32)).astype(jnp.bfloat16)
    return high, low


def dot(a, b):
    return jnp.dot(a, b, preferred_element_type=jnp.float32)


def sum_kernel(start, offset, first, last, n_base, meta, gradients, one, two, three, old_all, *refs):
    before = None if first else refs[0]
    outs = refs[(0 if first else 1) + n_base : -5]
    norms = None if last else outs[-1]
    outs = outs if last else outs[:-1]
    own, old, codes, in_sems, sems = refs[-5:]
    nbg, per, width = one.shape
    rows = pl.ds(start, per)
    loads = [
        pltpu.make_async_copy(gradients.at[0, pl.ds(meta[0] * nbg, nbg), rows], own, in_sems.at[0]),
        pltpu.make_async_copy(old_all.at[:, rows], old, in_sems.at[1]),
    ]
    for x in loads:
        x.start()
    for x in loads:
        x.wait()

    def code_block(at):
        total = (own[at].astype(jnp.float32) + one[at].astype(jnp.float32)) + (
            two[at].astype(jnp.float32) + three[at].astype(jnp.float32)
        )
        moment = 0.95 * old[at].astype(jnp.float32) + 0.05 * total * total
        adam = total / (moment * lax.rsqrt(moment) + 1e-08)
        adam = adam * adam
        parts = [total[:, j : j + LANES] for j in range(0, width, LANES)]
        top = functools.reduce(jnp.maximum, [jnp.abs(p) for p in parts])
        if last:
            top = jnp.maximum(top, pltpu.roll(top, 4, 0))
        power = jnp.floor(jnp.log2(jnp.maximum(top, 1e-30)) + 1e-4) - 14.0
        grow = jnp.exp2(-power)
        for j, p in enumerate(parts):
            codes[at, :, j * LANES : (j + 1) * LANES] = jnp.round(p * grow).astype(jnp.int32).astype(jnp.int16)
        squares = functools.reduce(jnp.add, [adam[:, j : j + LANES] for j in range(0, width, LANES)])
        squares = jnp.sum(squares, axis=0, keepdims=True)
        if not first:
            squares = squares + before[at]
        if not last:
            norms[at] = squares
            codes[at, :, width:] = power.astype(jnp.int32).astype(jnp.int16)
            return
        scale = jnp.ceil(jnp.log2(jnp.maximum(squares, 1e-30)))
        scaled = squares * jnp.exp2(14.0 - scale)
        high = jnp.floor(scaled)
        low = jnp.floor((scaled - high) * 16384.0)
        row = lax.broadcasted_iota(jnp.int32, power.shape, 0)
        full = jnp.where(row < 4, power, jnp.where(row == 4, scale, jnp.where(row == 5, high, low)))
        codes[at, :, width:] = full.astype(jnp.int32).astype(jnp.int16)

    def block(at, _):
        code_block(at)
        owner, rank = meta[1 + at], meta[1 + nbg + at]
        if len(outs) == 1:
            to = outs[0].at[owner, jnp.minimum(rank, outs[0].shape[1] - 1), to_rows]
            pltpu.make_async_copy(codes.at[at], to, sems.at[at]).start()
        else:
            for k, out in enumerate(outs):

                @pl.when(rank == k)
                def _():
                    pltpu.make_async_copy(codes.at[at], out.at[owner, to_rows], sems.at[at]).start()

        return 0

    to_rows = pl.ds(offset, per)
    lax.fori_loop(0, nbg, block, 0)
    done = outs[0].at[0, 0, to_rows] if len(outs) == 1 else outs[0].at[0, to_rows]
    for n in range(nbg):
        pltpu.make_async_copy(codes.at[n], done, sems.at[n]).wait()


def sum_replicas(gradients, received, old, start, meta, before, last, offset, shapes, base):
    nbg, per, width = received[0].shape
    columns = width + LANES
    out_shapes = [pltpu.HBM(x, jnp.int16) for x in shapes]
    if not last:
        out_shapes.append(jax.ShapeDtypeStruct((nbg, 1, LANES), jnp.float32))
    carried = [] if before is None else [before]
    base = [in_hbm(x) for x in base]
    return pl.pallas_call(
        functools.partial(sum_kernel, start, offset, before is None, last, len(base)),
        out_shape=out_shapes,
        in_specs=[SMEM, ANY, VMEM, VMEM, VMEM, ANY] + [VMEM] * len(carried) + [ANY] * len(base),
        out_specs=[ANY] * len(shapes) + ([] if last else [VMEM]),
        scratch_shapes=[
            pltpu.VMEM((nbg, per, width), jnp.bfloat16),
            pltpu.VMEM((nbg, per, width), jnp.bfloat16),
            pltpu.VMEM((nbg, per, columns), jnp.int16),
            pltpu.SemaphoreType.DMA((2,)),
            pltpu.SemaphoreType.DMA((nbg,)),
        ],
        input_output_aliases={6 + len(carried) + n: n for n in range(len(base))},
        compiler_params=SMALL,
    )(meta, in_hbm(gradients), *[in_vmem(r) for r in received], in_hbm(old), *carried, *base)


def owner_kernel(slot, all_roots, *refs):
    early, late, out, high, low, pre, roots, update, sems, out_sems = refs
    width = update.shape[0]
    loads = [pltpu.make_async_copy(all_roots.at[0, 0, slot, k], roots.at[k], sems.at[k]) for k in (1, 0)]
    for x in loads:
        x.start()
    n_src, per = late.shape[:2]
    rows = 2 * per

    def unpack(n, graft):
        codes = [early[n, slot], late[n]]
        tails = [x[:, width:].astype(jnp.int32).astype(jnp.float32) for x in codes]
        norm = tails[1][8:]
        row = lax.broadcasted_iota(jnp.int32, norm.shape, 0)
        tails[1] = jnp.concatenate([tails[1][:8], jnp.where(row < 4, norm, pltpu.roll(norm, 4, 0))], axis=0)
        for c, (code, tail) in enumerate(zip(codes, tails)):
            at = pl.ds(pl.multiple_of(n * rows + c * per, per), per)
            step = jnp.exp2(tail)
            for j in range(0, width, LANES):
                value = code[:, j : j + LANES].astype(jnp.int32).astype(jnp.float32) * step
                high[at, j : j + LANES], low[at, j : j + LANES] = two_parts(value)
        return graft + jnp.exp2(norm[4:5] - 14.0) * (norm[5:6] + norm[6:7] * (1.0 / 16384.0))

    graft = lax.fori_loop(0, n_src, unpack, jnp.zeros((1, LANES), jnp.float32))
    graft = jnp.sum(graft, axis=1, keepdims=True)
    loads[0].wait()
    right = roots[1]
    for m in range(0, width, TALL):
        at = pl.ds(m, TALL)
        high[at, :], low[at, :] = two_parts(dot(high[at, :], right) + dot(low[at, :], right))
    loads[1].wait()
    square = jnp.zeros((1, width), jnp.float32)
    for m in range(0, width, TALL):
        at = pl.ds(m, TALL)
        left = roots[0, at, :]
        got = dot(left, high[...]) + dot(left, low[...])
        pre[at, :] = got
        square = square + jnp.sum(got * got, axis=0, keepdims=True)
    square = jnp.sum(square, axis=1, keepdims=True)
    scale = jnp.sqrt(graft) / jnp.sqrt(square + 1e-06)
    copies = []
    for n, m in enumerate(range(0, width, TALL)):
        at = pl.ds(m, TALL)
        update[at, :] = (scale * pre[at, :]).astype(jnp.bfloat16)
        copies.append(pltpu.make_async_copy(update.at[at], out.at[at], out_sems.at[n]))
        copies[-1].start()
    for c in copies:
        c.wait()


def owner_work(roots, arrived, slot):
    width = roots.shape[-1]
    return pl.pallas_call(
        functools.partial(owner_kernel, slot),
        out_shape=pltpu.HBM((width, width), jnp.bfloat16),
        in_specs=[ANY] + [VMEM] * len(arrived),
        out_specs=ANY,
        scratch_shapes=[
            pltpu.VMEM((width, width), jnp.bfloat16),
            pltpu.VMEM((width, width), jnp.bfloat16),
            pltpu.VMEM((width, width), jnp.float32),
            pltpu.VMEM((2, width, width), jnp.bfloat16),
            pltpu.VMEM((width, width), jnp.bfloat16),
            pltpu.SemaphoreType.DMA((2,)),
            pltpu.SemaphoreType.DMA((width // TALL,)),
        ],
        compiler_params=LARGE,
    )(in_hbm(roots), *[in_vmem(a) for a in arrived])


def order_kernel(table, weights, out, sems):
    copies = [pltpu.make_async_copy(weights.at[table[j]], out.at[j], sems.at[j]) for j in range(out.shape[0])]
    for c in copies:
        c.start()
    for c in copies:
        c.wait()


def order_blocks(table, weights):
    count = table.shape[0]
    return pl.pallas_call(
        order_kernel,
        out_shape=pltpu.VMEM((count,) + weights.shape[1:], weights.dtype),
        in_specs=[SMEM, ANY],
        out_specs=VMEM,
        scratch_shapes=[pltpu.SemaphoreType.DMA((count,))],
        compiler_params=SMALL,
    )(table, in_hbm(weights))


def renew_kernel(first, slot, table, weights, back, *refs):
    made, outs, sems = refs[:-3], refs[-3:-1], refs[-1]
    half = outs[0].shape[0]

    def block(j):
        grad = back[table[j]].astype(jnp.float32)
        stepped = weights[first + j].astype(jnp.float32) - 0.5 * grad
        scale = lax.rsqrt(jnp.mean(stepped * stepped, axis=1, keepdims=True) + 1e-06)
        outs[j // half][j % half] = (stepped * scale).astype(jnp.bfloat16)

    def kept(j):
        return pltpu.make_async_copy(made[j // half].at[j % half], outs[j // half].at[j % half], sems.at[j])

    if not made:
        for j in range(2 * half):
            block(j)
        return
    for j in range(2 * half):
        pl.when(table[2 * half + j] != slot)(lambda: kept(j).start())
    for j in range(2 * half):
        pl.when(table[2 * half + j] == slot)(functools.partial(block, j))
    for j in range(2 * half):
        pl.when(table[2 * half + j] != slot)(lambda: kept(j).wait())


def ahead_kernel(first, table, weights, back, out_a, out_b, some_a, some_b, sems):
    renew_kernel(first, 0, table, weights, back, some_a, some_b, sems)
    copies = [
        pltpu.make_async_copy(x, out, sems.at[n]) for n, (x, out) in enumerate([(some_a, out_a), (some_b, out_b)])
    ]
    for c in copies:
        c.start()
    for c in copies:
        c.wait()


def renew(table, weights, back, first, slot, made=()):
    count = table.shape[0] // 2
    half = pltpu.VMEM((count // 2,) + weights.shape[1:], jnp.bfloat16)
    return pl.pallas_call(
        functools.partial(renew_kernel, first, slot),
        out_shape=(half, half),
        in_specs=[SMEM, VMEM, VMEM] + [ANY] * len(made),
        out_specs=(VMEM, VMEM),
        scratch_shapes=[pltpu.SemaphoreType.DMA((count,))],
        compiler_params=SMALL,
    )(table, in_vmem(weights), in_vmem(back), *[in_hbm(x) for x in made])


def renew_ahead(table, weights, back, first):
    count = table.shape[0] // 2
    shape = (count // 2,) + weights.shape[1:]
    return pl.pallas_call(
        functools.partial(ahead_kernel, first),
        out_shape=(pltpu.HBM(shape, jnp.bfloat16), pltpu.HBM(shape, jnp.bfloat16)),
        in_specs=[SMEM, VMEM, VMEM],
        out_specs=(ANY, ANY),
        scratch_shapes=[
            pltpu.VMEM(shape, jnp.bfloat16),
            pltpu.VMEM(shape, jnp.bfloat16),
            pltpu.SemaphoreType.DMA((2,)),
        ],
        compiler_params=SMALL,
    )(table, in_vmem(weights), in_vmem(back))


def pass_kernel(count, *refs):
    for ref, out in zip(refs[:count], refs[-count:]):
        for j in range(ref.shape[0]):
            out[j] = ref[j]


def pass_tables(tables, after=()):
    return pl.pallas_call(
        functools.partial(pass_kernel, len(tables)),
        out_shape=[jax.ShapeDtypeStruct(t.shape, t.dtype) for t in tables],
        in_specs=[SMEM] * len(tables) + [VMEM] * len(after),
        out_specs=[SMEM] * len(tables),
        compiler_params=SMALL,
    )(*tables, *[in_vmem(a) for a in after])


def scatter_kernel(place, *refs):
    pieces, out, sems = refs[:-2], refs[-2], refs[-1]
    copies = []
    for piece in pieces:
        for j in range(piece.shape[0]):
            n = len(copies)
            copies.append(pltpu.make_async_copy(piece.at[j], out.at[place[n]], sems.at[n]))
    for c in copies:
        c.start()
    for c in copies:
        c.wait()


def scatter_more_kernel(place, base, *refs):
    del base
    scatter_kernel(place, *refs)


def scatter_blocks(place, pieces, out_shape, base=None):
    pieces = [in_vmem(p) for p in pieces]
    count = sum(p.shape[0] for p in pieces)
    operands = pieces if base is None else [in_hbm(base)] + pieces
    return pl.pallas_call(
        scatter_kernel if base is None else scatter_more_kernel,
        out_shape=out_shape,
        in_specs=[SMEM] + [ANY] * (len(operands) - len(pieces)) + [pl.BlockSpec(memory_space=pltpu.VMEM)] * len(pieces),
        out_specs=ANY,
        scratch_shapes=[pltpu.SemaphoreType.DMA((count,))],
        input_output_aliases={} if base is None else {1: 0},
        compiler_params=SMALL,
    )(place, *operands)


def body(gradients, second_moment, inverse_roots, owners, weights):
    groups = lax.axis_size("groups")
    shards = lax.axis_size("shard")
    g = lax.axis_index("groups")
    total_blocks = owners.shape[0]
    nbg = total_blocks // groups
    slots = inverse_roots.shape[2]
    rows = gradients.shape[2]
    width = gradients.shape[3]
    half = nbg // 2

    def shift(n):
        return [(i, (i + n) % groups) for i in range(groups)]

    starts = [sum(CHUNKS[:c]) for c in range(len(CHUNKS))]
    received = []
    grads = gradients
    for start, per in zip(starts, CHUNKS):
        pieces = [
            lax.dynamic_slice(grads[0], (nbg * ((g + n) % groups), start, 0), (nbg, per, width)) for n in (1, 3, 2)
        ]
        grads, pieces = lax.optimization_barrier((grads, pieces))
        received.append([lax.ppermute(p, "groups", shift(n)) for p, n in zip(pieces, (1, 3, 2))])

    ids = jnp.arange(nbg, dtype=jnp.int32)
    earlier = ids[None, :] < ids[:, None]
    my_owner = lax.dynamic_slice_in_dim(owners, nbg * g, nbg)
    my_rank = jnp.sum(((my_owner[:, None] == my_owner[None, :]) & earlier).astype(jnp.int32), axis=1)
    meta = jnp.concatenate([g[None].astype(jnp.int32), my_owner, my_rank])
    grouped = owners.reshape(groups, nbg)
    same = grouped[:, :, None] == grouped[:, None, :]
    rank = jnp.sum((same & earlier[None]).astype(jnp.int32), axis=2)
    firsts = rank == 0
    before = jnp.sum((firsts[:, None, :] & earlier[None]).astype(jnp.int32), axis=2)
    n_first = jnp.sum(firsts.astype(jnp.int32), axis=1, keepdims=True)
    spot = jnp.where(firsts, before, n_first + ids[None] - before)
    sits = spot[:, None, :] == ids[None, :, None]
    order = jnp.sum(jnp.where(sits, ids[None, None, :], 0), axis=2)
    by_order = [
        lax.dynamic_index_in_dim(jnp.sum(jnp.where(sits, t[:, None, :], 0), axis=2), g, 0, False)
        for t in (jnp.broadcast_to(ids[None], grouped.shape), grouped, rank)
    ]

    def exchange(x, after=None):
        if after is not None:
            x, after = lax.optimization_barrier((x, after))
        return lax.all_to_all(x, "shard", 0, 0, tiled=True)

    columns = width + LANES
    norm = None
    coded = []
    for c in range(0, len(starts), 2):
        tall = CHUNKS[c] + CHUNKS[c + 1]
        final = c + 2 == len(starts)
        shapes = [(shards, tall, columns)] * slots if final else [(shards, slots, tall, columns)]
        code = []
        for d in (c, c + 1):
            last = final and d > c
            code = sum_replicas(
                gradients, received[d], second_moment, starts[d], meta, norm, last, starts[d] - starts[c], shapes, code
            )
            norm = None if last else code[-1]
            code = code[: len(shapes)]
        coded.append(code)
    early = exchange(coded[0][0])
    arrived = []
    for k in range(slots):
        arrived.append([early, exchange(coded[1][k], arrived[-1][-1] if k else early)])

    backs = []
    for k in range(slots):
        update = owner_work(inverse_roots, arrived[k], k)
        backs.append(exchange(update.reshape(shards, rows, width), backs[-1] if k else None))

    def to_all(new):
        a, b = new
        prev_a = lax.ppermute(a, "groups", shift(1))
        after_b = lax.ppermute(b, "groups", shift(3))
        prev_b = lax.ppermute(b, "groups", shift(1))
        after_a = lax.ppermute(a, "groups", shift(3))
        far_a = lax.ppermute(prev_a, "groups", shift(1))
        far_b = lax.ppermute(after_b, "groups", shift(3))
        return [a, b, prev_a, prev_b, after_a, after_b, far_a, far_b]

    def places(lo, hi):
        out = []
        for n in (0, 3, 1, 2):
            h = (g + n) % groups
            out.append(nbg * h + lax.dynamic_index_in_dim(order, h, 0, False)[lo:hi])
        return jnp.concatenate(out)

    def table(lo, hi):
        return jnp.concatenate([t[lo:hi] for t in by_order[1:]])

    out_shape = jax.ShapeDtypeStruct((total_blocks, rows, width), jnp.bfloat16)
    where = places(half, nbg)
    far = 3 * half
    tables = [table(0, half), table(half, nbg), places(0, half), where[:far], where[far:], by_order[0]]
    tables = pass_tables(tables)
    ordered = order_blocks(tables[5], weights)
    new = renew(tables[0], ordered, backs[0], 0, 0)
    pieces0 = to_all(new)
    late = pass_tables(tables[1:2], [pieces0[2], pieces0[5]])
    made = renew_ahead(late[0], ordered, backs[0], half)
    new = renew(late[0], ordered, backs[1], half, 1, made)
    pieces1 = to_all(new)
    out = scatter_blocks(tables[2], pieces0, out_shape)
    out = scatter_blocks(tables[3], pieces1[:6], out_shape, base=out)
    return scatter_blocks(tables[4], pieces1[6:], out_shape, base=out)


def solution(mesh):
    return jax.shard_map(
        body,
        mesh=mesh,
        in_specs=(
            P("groups", None, "shard", None),
            P("groups", "shard", None),
            P("groups", "shard", None, None, None, None),
            P(),
            P("groups", "shard", None),
        ),
        out_specs=P(None, "shard", None),
        check_vma=False,
    )
```
